32 devices in a mesh: atom: 16 (over z, y, x), wave: 2 (over core).
Axes of the slice: x: 2, y: 2, z: 4, core: 2. Of those that a mesh axis runs over, the one named last changes fastest.
Arguments:
- positions: float32 [3, 4096], P(None, ('atom', 'wave')), may hold values from 0 to 1
- counts: int32 [32], P(('atom', 'wave')), may hold values from 16 to 128, as said below
- feats: bfloat16 [4096, 256], P(('atom', 'wave')), may hold values from -6 to 6
- waves: int32 [3, 8192], P(None, 'wave'), may hold values from -12 to 12
- wave_filter: bfloat16 [8192, 256], P('wave'), may hold values from -5 to 5
- mixing: float32 [256, 256], replicated, may hold values from -0.375 to 0.375
- gain: float32 [256], replicated, may hold values from 0.1 to 1.9
- w_in: bfloat16 [256, 1024], replicated, may hold values from -0.375 to 0.375
- w_out: bfloat16 [1024, 256], replicated, may hold values from -0.1875 to 0.1875
Outputs:
- updated: bfloat16 [4096, 256], P(('atom', 'wave'))
The draws below stay inside these ranges and needn't reach their ends.
Inputs may be any that keep to these rules, and one draw needn't show every extreme that they name: `counts`: each block of 128 slots holds 16 to 128 live atoms at its start; every even-numbered block is full.
All inputs are finite; a program needn't handle non-finite values.
Results may differ from the reference program's by a relative error of at most 0.0055.
Values may be sent and summed in bfloat16 or wider, within the bound.
A program may use at most 128 MiB of HBM per device.

```python
import math
import jax
import jax.numpy as jnp
from jax import lax

C = 256
HID = 1024
KWAVES = 8192
ATOMS = 4096
BLOCKS = 32


def draw_counts(key, part):
    values = jax.random.randint(jax.random.fold_in(key, 11), (BLOCKS,), 16, 129)
    index = jnp.arange(BLOCKS, dtype=jnp.int32)
    return jnp.where(index % 2 == 0, 128, values).astype(jnp.int32)


def set_ends(drawn, rng, least, top_value):
    shape = drawn.shape
    place = [jax.random.randint(jax.random.fold_in(rng, axis), (), 0, shape[axis]) for axis in range(len(shape))]
    drawn = drawn.at[tuple(place)].set(least)
    longest = shape.index(max(shape))
    place[longest] = (place[longest] + 1) % shape[longest]
    return drawn.at[tuple(place)].set(top_value)


def levels(rng, shape, split, low, high):
    level, own = 1.0, jax.random.fold_in(rng, 6)
    for axis_at, parts in split:
        steps = jnp.exp(jax.random.uniform(jax.random.fold_in(own, axis_at), (parts,), jnp.float32, low / len(split), high / len(split)))
        level = level * jnp.repeat(steps, shape[axis_at] // parts).reshape([-1 if axis == axis_at else 1 for axis in range(len(shape))])
    return level


def normal_values(stream_key, extent, deviation, limit, split=(), kind=jnp.bfloat16):
    level = levels(stream_key, extent, split, -0.22, 0.18) if split else 1.0
    drawn = jax.random.normal(stream_key, extent, jnp.float32) * deviation * level
    return jnp.minimum(jnp.maximum(drawn, -limit), limit).astype(kind)


def setup_inputs(seed: int = 0) -> dict:
    seeds = jax.random.split(jax.random.key(seed), 10)
    positions = jnp.clip(1.0 * jax.random.uniform(seeds[0], (3, ATOMS), jnp.float32) ** levels(seeds[0], (3, ATOMS), ((1, 32),), -0.2, 0.2), 0.0, 1.0)
    counts = draw_counts(jax.random.fold_in(seeds[9], 71), 0)
    feats = normal_values(seeds[2], (ATOMS, C), 1.0, 6.0, ((0, 32),))
    waves = set_ends(jax.random.randint(seeds[3], (3, KWAVES), -12, 13), jax.random.fold_in(seeds[3], 1), -12, 12).astype(jnp.int32)
    wave_filter = normal_values(seeds[4], (KWAVES, C), 1.0, 5.0, ((0, 2),))
    mixing = normal_values(seeds[5], (C, C), C ** -0.5, 0.375, (), jnp.float32)
    gain = jnp.clip(1.0 + 0.18 * jax.random.normal(seeds[6], (C,), jnp.float32), 0.1, 1.9)
    w_in = normal_values(seeds[7], (C, HID), C ** -0.5, 0.375)
    w_out = normal_values(seeds[8], (HID, C), HID ** -0.5, 0.1875)
    return dict(positions=positions, counts=counts, feats=feats, waves=waves, wave_filter=wave_filter, mixing=mixing, gain=gain, w_in=w_in, w_out=w_out)


two_pi = 2.0 * math.pi

def phases(coords, wave_f):
    return (coords[0][:, None] * wave_f[0][None, :] + coords[1][:, None] * wave_f[1][None, :] + coords[2][:, None] * wave_f[2][None, :]) * two_pi

def reference(positions, counts, feats, waves, wave_filter, mixing, gain, w_in, w_out):
    slot = lax.broadcasted_iota(jnp.int32, (BLOCKS, 128), 1)
    live = (slot < counts[:, None]).reshape(ATOMS)
    masked = feats * live[:, None].astype(jnp.bfloat16)
    wave_f = waves.astype(jnp.float32)
    size = 512 if ATOMS % 512 == 0 else 128
    steps_n = ATOMS // size

    def forward(carry, index):
        start = (index * size).astype(jnp.int32)
        coords = lax.dynamic_slice_in_dim(positions, start, size, 1)
        rows_h = lax.dynamic_slice_in_dim(masked, start, size, 0)
        angle = phases(coords, wave_f)
        cosine = jnp.cos(angle).astype(jnp.bfloat16)
        sine = jnp.sin(angle).astype(jnp.bfloat16)
        real_add = jnp.dot(cosine.T, rows_h, preferred_element_type=jnp.float32)
        imag_add = jnp.dot(sine.T, rows_h, preferred_element_type=jnp.float32)
        return ((carry[0] + real_add, carry[1] + imag_add), None)
    zero = jnp.zeros((KWAVES, C), jnp.float32)
    (real_sum, imag_sum), _ = lax.scan(forward, (zero, zero), jnp.arange(steps_n, dtype=jnp.int32))
    scale = 1.0 / math.sqrt(ATOMS)
    filt = wave_filter.astype(jnp.float32)
    filtered_real = jnp.dot(real_sum * scale * filt, mixing, precision=lax.Precision.HIGHEST).astype(jnp.bfloat16)
    filtered_imag = jnp.dot(imag_sum * scale * filt, mixing, precision=lax.Precision.HIGHEST).astype(jnp.bfloat16)
    inv_k = 1.0 / math.sqrt(KWAVES)

    def inverse(index):
        start = (index * size).astype(jnp.int32)
        coords = lax.dynamic_slice_in_dim(positions, start, size, 1)
        angle = phases(coords, wave_f)
        cosine = jnp.cos(angle).astype(jnp.bfloat16)
        sine = jnp.sin(angle).astype(jnp.bfloat16)
        field = jnp.dot(cosine, filtered_real, preferred_element_type=jnp.float32) + jnp.dot(sine, filtered_imag, preferred_element_type=jnp.float32)
        return field * inv_k
    update = lax.map(inverse, jnp.arange(steps_n, dtype=jnp.int32)).reshape(ATOMS, C)
    state = feats.astype(jnp.float32) + update
    meansq = lax.optimization_barrier(jnp.mean(state * state, axis=1, keepdims=True))
    normed = (state * lax.rsqrt(meansq + 1e-06) * gain[None, :]).astype(jnp.bfloat16)
    hidden = jax.nn.silu(jnp.dot(normed, w_in, preferred_element_type=jnp.float32)).astype(jnp.bfloat16)
    result = state + jnp.dot(hidden, w_out, preferred_element_type=jnp.float32)
    return jnp.where(live[:, None], result, 0.0).astype(jnp.bfloat16)
```

```python
import functools
import math

import jax
import jax.numpy as jnp
from jax import lax
from jax.experimental import pallas as pl
from jax.experimental.pallas import tpu as pltpu
from jax.sharding import PartitionSpec as P

MESH = pl.DeviceIdType.MESH
BF, F32 = jnp.bfloat16, jnp.float32
HIGHEST = lax.Precision.HIGHEST
SIN = (4.442879586450294, -7.307818046861918, 3.5977887167859492, -0.7912381728222249)
COS = (1.414204080391997, -6.977642051264664, 5.715238335828671, -1.7283485048567975)
PARTS = 2


def horner(z, coefs):
    total = coefs[-1]
    for value in coefs[-2::-1]:
        total = total * z + value
    return total


def grid_of(n):
    side = 1
    while n % (4 * side * side) == 0 and 8 * side**3 <= n:
        side *= 2
    return n // (side * side), side


def kernel(
    n,
    planes,
    side,
    atoms_all,
    kwaves_all,
    counts_ref,
    pos_ref,
    feats_ref,
    waves_ref,
    filt_hbm,
    mixing_hbm,
    gain_ref,
    w_in_hbm,
    w_out_hbm,
    out_ref,
    filt_ref,
    filt_other,
    mixing_ref,
    w_in_ref,
    w_out_ref,
    stage,
    wave_own,
    wave_raw,
    pos_all,
    feat_all,
    wave_other,
    trig,
    factors,
    factors_out,
    factors_in,
    field_t,
    kept,
    send_u,
    recv_u,
    p_send,
    p_recv,
    f_send,
    f_recv,
    u_send,
    u_recv,
    c_send,
    c_recv,
    l_sem,
):
    kw, width = filt_ref.shape
    rows = feats_ref.shape[0]
    parts = feat_all.shape[0]
    wc = width // parts
    me = lax.axis_index("atom")
    core = lax.axis_index("wave")
    x = me % side
    y = (me // side) % side
    z = me // (side * side)
    b = y + core * (x - y)
    c = x + core * (y - x)
    stride_b = side + core * (1 - side)
    stride_c = 1 + core * (side - 1)

    def ident(dz, db, dc):
        return (dc * side + db) * planes + dz

    def ahead(dz, db, dc):
        zz, bb, cc = (z + dz) % planes, (b + db) % side, (c + dc) % side
        return (zz * (side * side) + bb * stride_b + cc * stride_c, core)

    def back(dz, db, dc):
        return ahead(planes - dz, side - db, side - dc)

    partner = (me, 1 - core)
    far = range(1, planes)
    near = [(db, dc) for dc in range(side) for db in range(side) if db or dc]
    every = [(dz, db, dc) for dc in range(side) for db in range(side) for dz in range(planes)][1:]

    barrier = pltpu.get_barrier_semaphore()
    for peer in [partner] + [ahead(*k) for k in every]:
        pl.semaphore_signal(barrier, inc=1, device_id=peer, device_id_type=MESH)

    local = [
        pltpu.make_async_copy(src, dst, l_sem.at[k])
        for k, (src, dst) in enumerate(
            (
                (filt_hbm.at[pl.ds(pl.multiple_of(me * kw, kw), kw)], filt_ref),
                (mixing_hbm, mixing_ref),
                (w_in_hbm, w_in_ref),
                (w_out_hbm, w_out_ref),
            )
        )
    ]
    for copy in local:
        copy.start()

    slot = lax.broadcasted_iota(jnp.int32, (rows, width), 0)
    live = slot < counts_ref[0]
    feats = feats_ref[...].astype(F32)
    masked = jnp.where(live, feats, 0.0).astype(BF)
    for h in range(parts):
        feat_all[h, 0] = masked[:, h * wc : (h + 1) * wc]
    place = pos_ref[...]
    high = place.astype(BF).astype(F32)
    middle = (place - high).astype(BF).astype(F32)
    stage[...] = jnp.zeros_like(stage)
    stage[0:3, :rows] = high
    stage[3:6, :rows] = middle
    stage[6:9, :rows] = place - high - middle
    pos_all[0] = stage[:, :rows].astype(BF)

    window = max(kw, 128)
    first = pl.multiple_of((me * kw) // window * window, window)
    shift = me * kw - first

    def turned(raw):
        for part in range(3):
            stage[3 * part : 3 * part + 3, :] = raw.astype(F32)
        found = stage[...]
        if kw < window:
            found = pltpu.roll(found, (window - shift) % window, 1)
        return found.T[:kw].astype(BF)

    sent = []

    def remote(src, dst, send, recv, peer):
        copy = pltpu.make_async_remote_copy(
            src_ref=src,
            dst_ref=dst,
            send_sem=send,
            recv_sem=recv,
            device_id=peer,
            device_id_type=MESH,
        )
        copy.start()
        sent.append(copy)
        return copy

    f_copies, u_copies = {}, {}

    def send_feat(h, src, dst, peer):
        f_copies[h, dst] = remote(
            feat_all.at[h, src], feat_all.at[h, dst], f_send.at[h, dst], f_recv.at[h, dst], peer
        )

    def spread(h, dz):
        for db, dc in near:
            send_feat(h, ident(dz, 0, 0), ident(dz, db, dc), ahead(0, db, dc))

    def begin(h):
        for dz in far:
            send_feat(h, 0, dz, ahead(dz, 0, 0))
        spread(h, 0)

    def forward(h):
        for dz in far:
            f_copies[h, dz].wait_recv()
            spread(h, dz)

    def core_copy(src, dst, k):
        return remote(src, dst, c_send.at[k], c_recv.at[k], partner)

    pl.semaphore_wait(barrier, n)
    begin(0)
    wave_copy = core_copy(waves_ref.at[:, pl.ds(first, window)], wave_raw, 0)
    p_copies = {}
    for k in every:
        i = ident(*k)
        p_copies[i] = remote(pos_all.at[0], pos_all.at[i], p_send.at[i], p_recv.at[i], ahead(*k))
    wave_own[...] = turned(waves_ref[:, pl.ds(first, window)])
    local[0].wait()
    filt_copy = core_copy(filt_ref, filt_other, 1)
    wave_copy.wait_recv()
    wave_other[...] = turned(wave_raw[...])

    block = min(kw, 128)
    group_cols = planes * rows

    def angles(g, lo, count):
        for k in range(g * planes + lo, g * planes + lo + count):
            if k:
                p_copies[k].wait_recv()
        base_k = g * planes + lo
        columns = slice(base_k * rows, (base_k + count) * rows)
        spots = jnp.concatenate([pos_all[base_k + d] for d in range(count)], axis=1)
        for half, ref in enumerate((wave_own, wave_other)):
            base = half * 2 * kw
            for r0 in range(0, kw, block):
                turns = jnp.dot(ref[r0 : r0 + block, :], spots, preferred_element_type=F32)
                r = turns - jnp.round(turns)
                zz = r * r
                s = r * horner(zz, SIN)
                co = horner(zz, COS)
                trig[base + r0 : base + r0 + block, columns] = (1.0 - s * s).astype(BF)
                trig[base + kw + r0 : base + kw + r0 + block, columns] = (s * co).astype(BF)

    step = min(4 * kw, 512)
    groups = side * side

    def part_sum(h, g, r0):
        columns = slice(g * group_cols, (g + 1) * group_cols)
        feats_g = feat_all[h, g * planes : (g + 1) * planes].reshape(group_cols, wc)
        return jnp.dot(trig[r0 : r0 + step, columns], feats_g, preferred_element_type=F32)

    def sums(h, g):
        for k in range(max(g * planes, planes), (g + 1) * planes):
            f_copies[h, k].wait_recv()
        for r0 in range(0, 4 * kw, step):
            part = part_sum(h, g, r0)
            if g:
                part = factors[h, r0 : r0 + step, :] + part
            factors[h, r0 : r0 + step, :] = part
            if g == groups - 1:
                factors_out[h, r0 : r0 + step, :] = part.astype(BF)

    def exchange(h):
        return [
            core_copy(
                factors_out.at[h, pl.ds((1 - half) * 2 * kw, 2 * kw)],
                factors_in.at[h, pl.ds(half * 2 * kw, 2 * kw)],
                2 + 2 * h + half,
            )
            for half in range(2)
        ]

    scale = 1.0 / math.sqrt(atoms_all)

    def fields(h, swaps):
        for half, ref in enumerate((filt_ref, filt_other)):
            swaps[half].wait_recv()
            filt = ref[:, h * wc : (h + 1) * wc].astype(F32) * scale
            for part in range(2):
                r0 = (2 * half + part) * kw
                total = factors[h, r0 : r0 + kw, :] + factors_in[h, r0 : r0 + kw, :].astype(F32)
                field_t[h, :, r0 : r0 + kw] = (total * filt).T.astype(BF)

    inv_k = 1.0 / math.sqrt(kwaves_all)
    pair = 2

    def start_u(h, i, peer):
        u_copies[h, i] = remote(
            send_u.at[h, i], recv_u.at[h, i], u_send.at[h, i], u_recv.at[h, i], peer
        )

    def received(h, i):
        u_copies[h, i].wait_recv()
        return recv_u[h, i].astype(F32)

    def update(h, dz, db, dc):
        i = ident(dz, db, dc)
        both = jnp.dot(
            field_t[h], trig[:, i * rows : (i + pair) * rows], preferred_element_type=F32
        )
        for d in range(pair):
            block_d = both[:, d * rows : (d + 1) * rows]
            if db or dc:
                send_u[h, i + d] = block_d.astype(BF)
                start_u(h, i + d, back(0, db, dc))
            else:
                kept[h, dz + d] = block_d

    zorder = list(range(planes - pair, -1, -pair))

    def push(h):
        for dz in zorder:
            for db, dc in near:
                update(h, dz, db, dc)
        for dz in zorder:
            update(h, dz, 0, 0)

    def plane_sum(h, dz):
        acc = kept[h, dz]
        for db, dc in near:
            acc = acc + received(h, ident(dz, db, dc))
        return acc

    def columns_out(h):
        for start in zorder:
            for dz in range(start, start + pair):
                if dz:
                    send_u[h, dz] = plane_sum(h, dz).astype(BF)
                    start_u(h, dz, back(dz, 0, 0))

    def mine(h):
        acc = plane_sum(h, 0)
        for dz in far:
            acc = acc + received(h, dz)
        return acc

    angles(0, 0, 1)
    forward(0)
    for h in range(1, parts):
        begin(h)
    angles(0, 1, planes - 1)
    for h in range(1, parts):
        forward(h)
    for g in range(1, groups):
        for lo in range(0, planes, 2):
            angles(g, lo, 2)
    swaps = []
    for h in range(parts):
        for g in range(groups):
            sums(h, g)
        swaps.append(exchange(h))
        if h == 0:
            for copy in local[1:]:
                copy.wait()
            filt_copy.wait_recv()
        fields(h, swaps[h])
        push(h)
    for h in range(parts):
        columns_out(h)
    gathered = jnp.concatenate([mine(h) for h in range(parts)], axis=0)
    mixed = jnp.dot(gathered.T, mixing_ref[...], precision=HIGHEST, preferred_element_type=F32)

    state = feats + mixed * inv_k
    meansq = jnp.mean(state * state, axis=1, keepdims=True)
    normed = (state * lax.rsqrt(meansq + 1e-06) * gain_ref[...].reshape(1, width)).astype(BF)
    inner = jnp.dot(normed, w_in_ref[...], preferred_element_type=F32)
    hidden = (inner / (1.0 + jnp.exp(-inner))).astype(BF)
    result = state + jnp.dot(hidden, w_out_ref[...], preferred_element_type=F32)
    out_ref[...] = jnp.where(live, result, 0.0)

    for copy in sent:
        copy.wait_send()


def body(n, cores, positions, counts, feats, waves, wave_filter, mixing, gain, w_in, w_out):
    rows, width = feats.shape
    planes, side = grid_of(n)
    kwaves_all = waves.shape[1] * cores
    kw = waves.shape[1] // n
    wc = width // PARTS
    vmem = pl.BlockSpec(memory_space=pltpu.VMEM)
    hbm = pl.BlockSpec(memory_space=pl.ANY)
    return pl.pallas_call(
        functools.partial(kernel, n, planes, side, rows * n * cores, kwaves_all),
        out_shape=jax.ShapeDtypeStruct((rows, width), F32),
        in_specs=[pl.BlockSpec(memory_space=pltpu.SMEM)]
        + [vmem] * 3
        + [hbm] * 2
        + [vmem]
        + [hbm] * 2,
        out_specs=vmem,
        scratch_shapes=[
            pltpu.VMEM((kw, width), BF),
            pltpu.VMEM((kw, width), BF),
            pltpu.VMEM(mixing.shape, F32),
            pltpu.VMEM(w_in.shape, BF),
            pltpu.VMEM(w_out.shape, BF),
            pltpu.VMEM((16, max(kw, 128)), F32),
            pltpu.VMEM((kw, 16), BF),
            pltpu.VMEM((3, max(kw, 128)), waves.dtype),
            pltpu.VMEM((n, 16, rows), BF),
            pltpu.VMEM((PARTS, n, rows, wc), BF),
            pltpu.VMEM((kw, 16), BF),
            pltpu.VMEM((4 * kw, n * rows), BF),
            pltpu.VMEM((PARTS, 4 * kw, wc), F32),
            pltpu.VMEM((PARTS, 4 * kw, wc), BF),
            pltpu.VMEM((PARTS, 4 * kw, wc), BF),
            pltpu.VMEM((PARTS, wc, 4 * kw), BF),
            pltpu.VMEM((PARTS, planes, wc, rows), F32),
            pltpu.VMEM((PARTS, n, wc, rows), BF),
            pltpu.VMEM((PARTS, n, wc, rows), BF),
        ]
        + [pltpu.SemaphoreType.DMA((n,))] * 2
        + [pltpu.SemaphoreType.DMA((PARTS, n))] * 4
        + [pltpu.SemaphoreType.DMA((2 + 2 * PARTS,))] * 2
        + [pltpu.SemaphoreType.DMA((4,))],
        compiler_params=pltpu.CompilerParams(
            collective_id=0, has_side_effects=True, vmem_limit_bytes=60 * 2**20
        ),
    )(counts, positions, feats, waves, wave_filter, mixing, gain, w_in, w_out).astype(BF)


def solution(mesh):
    n, cores = mesh.shape["atom"], mesh.shape["wave"]
    return jax.shard_map(
        functools.partial(body, n, cores),
        mesh=mesh,
        in_specs=(
            P(None, ("atom", "wave")),
            P(("atom", "wave")),
            P(("atom", "wave"), None),
            P(None, "wave"),
            P("wave", None),
            P(),
            P(),
            P(),
            P(),
        ),
        out_specs=P(("atom", "wave"), None),
        check_vma=False,
    )
```

```python
import functools
import math

import jax
import jax.numpy as jnp
from jax import lax
from jax.experimental import pallas as pl
from jax.experimental.pallas import tpu as pltpu
from jax.sharding import PartitionSpec as P

MESH = pl.DeviceIdType.MESH
BF, F32 = jnp.bfloat16, jnp.float32
HIGHEST = lax.Precision.HIGHEST
SIN = (4.442879586450294, -7.307818046861918, 3.5977887167859492, -0.7912381728222249)
COS = (1.414204080391997, -6.977642051264664, 5.715238335828671, -1.7283485048567975)
PARTS = 1


def horner(z, coefs):
    total = coefs[-1]
    for value in coefs[-2::-1]:
        total = total * z + value
    return total


def grid_of(n):
    side = 1
    while n % (4 * side * side) == 0 and 8 * side**3 <= n:
        side *= 2
    return n // (side * side), side


def kernel(
    n,
    planes,
    side,
    atoms_all,
    kwaves_all,
    counts_ref,
    pos_hbm,
    feats_hbm,
    waves_hbm,
    filt_hbm,
    mixing_hbm,
    gain_hbm,
    w_in_hbm,
    w_out_hbm,
    out_ref,
    pos_ref,
    feats_ref,
    waves_ref,
    gain_ref,
    filt_ref,
    filt_other,
    mixing_ref,
    w_in_ref,
    w_out_ref,
    stage,
    wave_own,
    wave_raw,
    pos_all,
    feat_all,
    wave_other,
    trig,
    factors,
    factors_out,
    factors_in,
    field_t,
    kept,
    send_u,
    recv_u,
    p_send,
    p_recv,
    f_send,
    f_recv,
    u_send,
    u_recv,
    c_send,
    c_recv,
    l_sem,
):
    kw, width = filt_ref.shape
    rows = feats_ref.shape[0]
    parts = feat_all.shape[0]
    wc = width // parts
    me = lax.axis_index("atom")
    core = lax.axis_index("wave")
    x = me % side
    y = (me // side) % side
    z = me // (side * side)
    b = y + core * (x - y)
    c = x + core * (y - x)
    stride_b = side + core * (1 - side)
    stride_c = 1 + core * (side - 1)

    def ident(dz, db, dc):
        return (dz * side + dc) * side + db

    def crossed(value, mask):
        bit = 1
        while bit <= mask:
            if mask & bit:
                value = value + bit * (1 - 2 * ((value // bit) % 2))
            bit *= 2
        return value

    def ahead(dz, db, dc):
        zz, bb, cc = crossed(z, dz), (b + db) % side, (c + dc) % side
        return (zz * (side * side) + bb * stride_b + cc * stride_c, core)

    def back(dz, db, dc):
        return ahead(dz, side - db, side - dc)

    partner = (me, 1 - core)
    far = range(2, planes)
    near = [(db, dc) for dc in range(side) for db in range(side) if db or dc]
    every = [(dz, db, dc) for dz in range(planes) for dc in range(side) for db in range(side)][1:]
    flat = side * side

    barrier = pltpu.get_barrier_semaphore()
    for peer in [partner] + [ahead(*k) for k in every]:
        pl.semaphore_signal(barrier, inc=1, device_id=peer, device_id_type=MESH)

    window = max(kw, 128)
    first = pl.multiple_of((me * kw) // window * window, window)
    shift = me * kw - first
    local = [
        pltpu.make_async_copy(src, dst, l_sem.at[k])
        for k, (src, dst) in enumerate(
            (
                (feats_hbm, feats_ref),
                (pos_hbm, pos_ref),
                (waves_hbm.at[:, pl.ds(first, window)], waves_ref),
                (filt_hbm.at[pl.ds(pl.multiple_of(me * kw, kw), kw)], filt_ref),
                (mixing_hbm, mixing_ref),
                (w_in_hbm, w_in_ref),
                (w_out_hbm, w_out_ref),
                (gain_hbm, gain_ref),
            )
        )
    ]
    for copy in local:
        copy.start()

    local[0].wait()
    slot = lax.broadcasted_iota(jnp.int32, (rows, width), 0)
    live = slot < counts_ref[0]
    feats = feats_ref[...].astype(F32)
    masked = jnp.where(live, feats, 0.0).astype(BF)
    for h in range(parts):
        feat_all[h, 0] = masked[:, h * wc : (h + 1) * wc]
    local[1].wait()
    place = pos_ref[...]
    high = place.astype(BF).astype(F32)
    middle = (place - high).astype(BF).astype(F32)
    stage[...] = jnp.zeros_like(stage)
    stage[0:3, :rows] = high
    stage[3:6, :rows] = middle
    stage[6:9, :rows] = place - high - middle
    pos_all[0] = stage[:, :rows].astype(BF)

    def turned(raw):
        for part in range(3):
            stage[3 * part : 3 * part + 3, :] = raw.astype(F32)
        found = stage[...]
        if kw < window:
            found = pltpu.roll(found, (window - shift) % window, 1)
        return found.T[:kw].astype(BF)

    sent = []

    def remote(src, dst, send, recv, peer):
        copy = pltpu.make_async_remote_copy(
            src_ref=src,
            dst_ref=dst,
            send_sem=send,
            recv_sem=recv,
            device_id=peer,
            device_id_type=MESH,
        )
        copy.start()
        sent.append(copy)
        return copy

    f_copies, u_copies = {}, {}

    def send_feat(h, src, dst, peer):
        f_copies[h, dst] = remote(
            feat_all.at[h, src], feat_all.at[h, dst], f_send.at[h, dst], f_recv.at[h, dst], peer
        )

    def begin(h):
        for dz in range(1, planes):
            send_feat(h, 0, dz * flat, ahead(dz, 0, 0))
        spread(h, 0)

    def spread(h, dz):
        if dz:
            f_copies[h, dz * flat].wait_recv()
        for db, dc in near:
            send_feat(h, ident(dz, 0, 0), ident(dz, db, dc), ahead(0, db, dc))

    def across(h):
        for db, dc in near:
            f_copies[h, ident(0, db, dc)].wait_recv()
            send_feat(h, ident(0, db, dc), ident(1, db, dc), ahead(1, 0, 0))

    def core_copy(src, dst, k):
        return remote(src, dst, c_send.at[k], c_recv.at[k], partner)

    pl.semaphore_wait(barrier, n)
    begin(0)
    local[2].wait()
    wave_copy = core_copy(waves_ref, wave_raw, 0)
    p_copies = {}
    for k in every:
        i = ident(*k)
        p_copies[i] = remote(pos_all.at[0], pos_all.at[i], p_send.at[i], p_recv.at[i], ahead(*k))
    wave_own[...] = turned(waves_ref[...])
    local[3].wait()
    filt_copy = core_copy(filt_ref, filt_other, 1)
    wave_copy.wait_recv()
    wave_other[...] = turned(wave_raw[...])

    block = min(kw, 128)
    group_cols = flat * rows

    def angles(start, count):
        for k in range(start, start + count):
            if k:
                p_copies[k].wait_recv()
        columns = slice(start * rows, (start + count) * rows)
        spots = jnp.concatenate([pos_all[start + d] for d in range(count)], axis=1)
        for half, ref in enumerate((wave_own, wave_other)):
            base = half * 2 * kw
            for r0 in range(0, kw, block):
                turns = jnp.dot(ref[r0 : r0 + block, :], spots, preferred_element_type=F32)
                r = turns - jnp.round(turns)
                zz = r * r
                s = r * horner(zz, SIN)
                co = horner(zz, COS)
                trig[base + r0 : base + r0 + block, columns] = (1.0 - s * s).astype(BF)
                trig[base + kw + r0 : base + kw + r0 + block, columns] = (s * co).astype(BF)

    step = min(2 * kw, 512)
    def part_sum(h, g, r0):
        columns = slice(g * group_cols, (g + 1) * group_cols)
        feats_g = feat_all[h, g * flat : (g + 1) * flat].reshape(group_cols, wc)
        return jnp.dot(trig[r0 : r0 + step, columns], feats_g, preferred_element_type=F32)

    def sums(h, g):
        for k in range(g * flat + (g != 1), (g + 1) * flat):
            if g == 1 or (g and k % flat):
                f_copies[h, k].wait_recv()
        swaps = []
        for r0 in range(0, 4 * kw, step):
            part = part_sum(h, g, r0)
            if g:
                part = factors[h, r0 : r0 + step, :] + part
            factors[h, r0 : r0 + step, :] = part
            if g == planes - 1:
                factors_out[h, r0 : r0 + step, :] = part.astype(BF)
                if (r0 + step) % (2 * kw) == 0:
                    half = r0 // (2 * kw)
                    swaps += [
                        core_copy(
                            factors_out.at[h, pl.ds(half_k * 2 * kw, 2 * kw)],
                            factors_in.at[h, pl.ds((1 - half_k) * 2 * kw, 2 * kw)],
                            2 + 2 * h + half_k,
                        )
                        for half_k in (half,)
                    ]
        return swaps

    scale = 1.0 / math.sqrt(atoms_all)

    def fields(h, swaps):
        for half, ref in enumerate((filt_ref, filt_other)):
            swaps[1 - half].wait_recv()
            filt = ref[:, h * wc : (h + 1) * wc].astype(F32) * scale
            for part in range(2):
                r0 = (2 * half + part) * kw
                total = factors[h, r0 : r0 + kw, :] + factors_in[h, r0 : r0 + kw, :].astype(F32)
                field_t[h, :, r0 : r0 + kw] = (total * filt).astype(BF).T

    inv_k = 1.0 / math.sqrt(kwaves_all)
    pair = 2

    def start_u(h, i, peer):
        u_copies[h, i] = remote(
            send_u.at[h, i], recv_u.at[h, i], u_send.at[h, i], u_recv.at[h, i], peer
        )

    def received(h, i):
        u_copies[h, i].wait_recv()
        return recv_u[h, i].astype(F32)

    def update(h, i):
        both = jnp.dot(
            field_t[h], trig[:, i * rows : (i + pair) * rows], preferred_element_type=F32
        )
        for k in range(i, i + pair):
            dz, dc, db = k // flat, k // side % side, k % side
            block_k = both[:, (k - i) * rows : (k - i + 1) * rows]
            if dz == 1 or (dz and (db or dc)):
                send_u[h, k] = block_k.astype(BF)
                start_u(h, k, back(1, 0, 0) if dz == 1 else back(0, db, dc))
            else:
                kept[h, flat + dz if dz else k] = block_k

    def push(h):
        for k in range(0, flat, pair):
            update(h, flat + k)
            update(h, 2 * flat + k)
        for k in range(3 * flat, n, pair):
            update(h, k)
        for k in range(0, flat, pair):
            update(h, k)

    def edges_out(h):
        for db, dc in near:
            i = ident(0, db, dc)
            acc = kept[h, i] + received(h, flat + i)
            send_u[h, i] = acc.astype(BF)
            start_u(h, i, back(0, db, dc))

    def columns_out(h):
        for dz in far:
            acc = kept[h, flat + dz]
            for db, dc in near:
                acc = acc + received(h, ident(dz, db, dc))
            send_u[h, dz * flat] = acc.astype(BF)
            start_u(h, dz * flat, back(dz, 0, 0))

    def mine(h):
        acc = kept[h, 0] + received(h, flat)
        for db, dc in near:
            acc = acc + received(h, ident(0, db, dc))
        for dz in far:
            acc = acc + received(h, dz * flat)
        return acc

    for h in range(1, parts):
        begin(h)
    angles(0, 1)
    for h in range(parts):
        across(h)
        for dz in far:
            spread(h, dz)
    angles(1, 1)
    for k in range(pair, n, pair):
        angles(k, pair)
    for copy in local[4:]:
        copy.wait()
    filt_copy.wait_recv()
    for h in range(parts):
        for g in range(planes):
            swaps = sums(h, g)
        fields(h, swaps)
        push(h)
    for h in range(parts):
        edges_out(h)
        columns_out(h)
    gathered = jnp.concatenate([mine(h) for h in range(parts)], axis=0)
    mixed = jnp.dot(gathered.T, mixing_ref[...], precision=HIGHEST, preferred_element_type=F32)

    state = feats + mixed * inv_k
    meansq = jnp.mean(state * state, axis=1, keepdims=True)
    normed = (state * lax.rsqrt(meansq + 1e-06) * gain_ref[...].reshape(1, width)).astype(BF)
    inner = jnp.dot(normed, w_in_ref[...], preferred_element_type=F32)
    hidden = (inner / (1.0 + jnp.exp(-inner))).astype(BF)
    result = state + jnp.dot(hidden, w_out_ref[...], preferred_element_type=F32)
    out_ref[...] = jnp.where(live, result, 0.0)

    for copy in sent:
        copy.wait_send()


def body(n, cores, positions, counts, feats, waves, wave_filter, mixing, gain, w_in, w_out):
    rows, width = feats.shape
    planes, side = grid_of(n)
    kwaves_all = waves.shape[1] * cores
    kw = waves.shape[1] // n
    wc = width // PARTS
    vmem = pl.BlockSpec(memory_space=pltpu.VMEM)
    hbm = pl.BlockSpec(memory_space=pltpu.HBM)
    held = [
        pltpu.with_memory_space_constraint(array, pltpu.HBM)
        for array in (positions, feats, waves, wave_filter, mixing, gain, w_in, w_out)
    ]
    return pl.pallas_call(
        functools.partial(kernel, n, planes, side, rows * n * cores, kwaves_all),
        out_shape=pltpu.VMEM((rows, width), F32),
        in_specs=[pl.BlockSpec(memory_space=pltpu.SMEM)]
        + [hbm] * 8,
        out_specs=vmem,
        scratch_shapes=[
            pltpu.VMEM(positions.shape, F32),
            pltpu.VMEM(feats.shape, BF),
            pltpu.VMEM((3, max(kw, 128)), waves.dtype),
            pltpu.VMEM(gain.shape, F32),
            pltpu.VMEM((kw, width), BF),
            pltpu.VMEM((kw, width), BF),
            pltpu.VMEM(mixing.shape, F32),
            pltpu.VMEM(w_in.shape, BF),
            pltpu.VMEM(w_out.shape, BF),
            pltpu.VMEM((16, max(kw, 128)), F32),
            pltpu.VMEM((kw, 16), BF),
            pltpu.VMEM((3, max(kw, 128)), waves.dtype),
            pltpu.VMEM((n, 16, rows), BF),
            pltpu.VMEM((PARTS, n, rows, wc), BF),
            pltpu.VMEM((kw, 16), BF),
            pltpu.VMEM((4 * kw, n * rows), BF),
            pltpu.VMEM((PARTS, 4 * kw, wc), F32),
            pltpu.VMEM((PARTS, 4 * kw, wc), BF),
            pltpu.VMEM((PARTS, 4 * kw, wc), BF),
            pltpu.VMEM((PARTS, wc, 4 * kw), BF),
            pltpu.VMEM((PARTS, planes + side * side, wc, rows), F32),
            pltpu.VMEM((PARTS, n, wc, rows), BF),
            pltpu.VMEM((PARTS, n, wc, rows), BF),
        ]
        + [pltpu.SemaphoreType.DMA((n,))] * 2
        + [pltpu.SemaphoreType.DMA((PARTS, n))] * 4
        + [pltpu.SemaphoreType.DMA((2 + 2 * PARTS,))] * 2
        + [pltpu.SemaphoreType.DMA((8,))],
        compiler_params=pltpu.CompilerParams(
            collective_id=0, has_side_effects=True, vmem_limit_bytes=48 * 2**20
        ),
    )(counts, *held).astype(BF)


def solution(mesh):
    n, cores = mesh.shape["atom"], mesh.shape["wave"]
    return jax.shard_map(
        functools.partial(body, n, cores),
        mesh=mesh,
        in_specs=(
            P(None, ("atom", "wave")),
            P(("atom", "wave")),
            P(("atom", "wave"), None),
            P(None, "wave"),
            P("wave", None),
            P(),
            P(),
            P(),
            P(),
        ),
        out_specs=P(("atom", "wave"), None),
        check_vma=False,
    )
```

```python
import functools
import math

import jax
import jax.numpy as jnp
from jax import lax
from jax.experimental import pallas as pl
from jax.experimental.pallas import tpu as pltpu
from jax.sharding import PartitionSpec as P

MESH = pl.DeviceIdType.MESH
BF, F32 = jnp.bfloat16, jnp.float32
HIGHEST = lax.Precision.HIGHEST
SIN = (4.442879586450294, -7.307818046861918, 3.5977887167859492, -0.7912381728222249)
COS = (1.414204080391997, -6.977642051264664, 5.715238335828671, -1.7283485048567975)
PARTS = 1


def horner(z, coefs):
    total = coefs[-1]
    for value in coefs[-2::-1]:
        total = total * z + value
    return total


def grid_of(n):
    side = 1
    while n % (4 * side * side) == 0 and 8 * side**3 <= n:
        side *= 2
    return n // (side * side), side


def kernel(
    n,
    planes,
    side,
    atoms_all,
    kwaves_all,
    counts_ref,
    pos_hbm,
    feats_hbm,
    waves_hbm,
    filt_hbm,
    mixing_hbm,
    gain_hbm,
    w_in_hbm,
    w_out_hbm,
    out_ref,
    pos_ref,
    feats_ref,
    waves_ref,
    gain_ref,
    filt_ref,
    filt_other,
    mixing_ref,
    w_in_ref,
    w_out_ref,
    stage,
    wave_own,
    wave_raw,
    pos_all,
    feat_all,
    wave_other,
    trig,
    factors,
    factors_out,
    factors_in,
    field_t,
    kept,
    send_u,
    recv_u,
    p_send,
    p_recv,
    f_send,
    f_recv,
    u_send,
    u_recv,
    c_send,
    c_recv,
    l_sem,
):
    kw, width = filt_ref.shape
    rows = feats_ref.shape[0]
    parts = feat_all.shape[0]
    wc = width // parts
    me = lax.axis_index("atom")
    core = lax.axis_index("wave")
    x = me % side
    y = (me // side) % side
    z = me // (side * side)
    b = y + core * (x - y)
    c = x + core * (y - x)
    stride_b = side + core * (1 - side)
    stride_c = 1 + core * (side - 1)

    def ident(dz, db, dc):
        return (dz * side + dc) * side + db

    def crossed(value, mask):
        bit = 1
        while bit <= mask:
            if mask & bit:
                value = value + bit * (1 - 2 * ((value // bit) % 2))
            bit *= 2
        return value

    def ahead(dz, db, dc):
        zz, bb, cc = crossed(z, dz), (b + db) % side, (c + dc) % side
        return (zz * (side * side) + bb * stride_b + cc * stride_c, core)

    def back(dz, db, dc):
        return ahead(dz, side - db, side - dc)

    partner = (me, 1 - core)
    far = range(2, planes)
    near = [(db, dc) for dc in range(side) for db in range(side) if db or dc]
    every = [(dz, db, dc) for dz in range(planes) for dc in range(side) for db in range(side)][1:]
    flat = side * side

    barrier = pltpu.get_barrier_semaphore()
    peers = [partner] + [ahead(dz, 0, 0) for dz in range(1, planes)]
    peers += [ahead(0, db, dc) for db, dc in near]
    for peer in peers:
        pl.semaphore_signal(barrier, inc=1, device_id=peer, device_id_type=MESH)

    window = max(kw, 128)
    first = pl.multiple_of((me * kw) // window * window, window)
    shift = me * kw - first
    local = [
        pltpu.make_async_copy(src, dst, l_sem.at[k])
        for k, (src, dst) in enumerate(
            (
                (feats_hbm, feats_ref),
                (pos_hbm, pos_ref),
                (waves_hbm.at[:, pl.ds(first, window)], waves_ref),
                (filt_hbm.at[pl.ds(pl.multiple_of(me * kw, kw), kw)], filt_ref),
                (mixing_hbm, mixing_ref),
                (w_in_hbm, w_in_ref),
                (w_out_hbm, w_out_ref),
                (gain_hbm, gain_ref),
            )
        )
    ]
    for copy in local:
        copy.start()

    local[0].wait()
    slot = lax.broadcasted_iota(jnp.int32, (rows, width), 0)
    live = slot < counts_ref[0]
    feats = feats_ref[...].astype(F32)
    masked = jnp.where(live, feats, 0.0).astype(BF)
    for h in range(parts):
        feat_all[h, 0] = masked[:, h * wc : (h + 1) * wc]
    local[1].wait()
    place = pos_ref[...]
    high = place.astype(BF).astype(F32)
    middle = (place - high).astype(BF).astype(F32)
    stage[...] = jnp.zeros_like(stage)
    stage[0:3, :rows] = high
    stage[3:6, :rows] = middle
    stage[6:9, :rows] = place - high - middle
    pos_all[0] = stage[:, :rows].astype(BF)

    def turned(raw):
        for part in range(3):
            stage[3 * part : 3 * part + 3, :] = raw.astype(F32)
        found = stage[...]
        if kw < window:
            found = pltpu.roll(found, (window - shift) % window, 1)
        return found.T[:kw].astype(BF)

    sent = []

    def remote(src, dst, send, recv, peer):
        copy = pltpu.make_async_remote_copy(
            src_ref=src,
            dst_ref=dst,
            send_sem=send,
            recv_sem=recv,
            device_id=peer,
            device_id_type=MESH,
        )
        copy.start()
        sent.append(copy)
        return copy

    f_copies, u_copies, p_copies = {}, {}, {}

    def send_place(src, dst, peer):
        p_copies[dst] = remote(
            pos_all.at[src], pos_all.at[dst], p_send.at[dst], p_recv.at[dst], peer
        )

    def p_begin():
        for dz in range(1, planes):
            send_place(0, dz * flat, ahead(dz, 0, 0))
        for db, dc in near:
            send_place(0, ident(0, db, dc), ahead(0, db, dc))

    def p_forward():
        for db, dc in near:
            i = ident(0, db, dc)
            p_copies[i].wait_recv()
            send_place(i, flat + i, ahead(1, 0, 0))
        for dz in far:
            p_copies[dz * flat].wait_recv()
            for db, dc in near:
                send_place(dz * flat, ident(dz, db, dc), ahead(0, db, dc))

    def send_feat(h, src, dst, peer):
        f_copies[h, dst] = remote(
            feat_all.at[h, src], feat_all.at[h, dst], f_send.at[h, dst], f_recv.at[h, dst], peer
        )

    def begin(h):
        spread(h, 0)
        for dz in (*far, 1):
            send_feat(h, 0, dz * flat, ahead(dz, 0, 0))

    def spread(h, dz):
        if dz:
            f_copies[h, dz * flat].wait_recv()
        for db, dc in near:
            send_feat(h, ident(dz, 0, 0), ident(dz, db, dc), ahead(0, db, dc))

    def across(h):
        for db, dc in near:
            f_copies[h, ident(0, db, dc)].wait_recv()
            send_feat(h, ident(0, db, dc), ident(1, db, dc), ahead(1, 0, 0))

    def core_copy(src, dst, k):
        return remote(src, dst, c_send.at[k], c_recv.at[k], partner)

    pl.semaphore_wait(barrier, len(peers))
    p_begin()
    begin(0)
    local[2].wait()
    wave_copy = core_copy(waves_ref, wave_raw, 0)
    wave_own[...] = turned(waves_ref[...])
    local[3].wait()
    filt_copy = core_copy(filt_ref, filt_other, 1)
    wave_copy.wait_recv()
    wave_other[...] = turned(wave_raw[...])

    block = min(kw, 128)
    group_cols = flat * rows

    def angles(start, count):
        for k in range(start, start + count):
            if k == flat or (k > flat and k % flat):
                p_copies[k].wait_recv()
        columns = slice(start * rows, (start + count) * rows)
        spots = jnp.concatenate([pos_all[start + d] for d in range(count)], axis=1)
        for half, ref in enumerate((wave_own, wave_other)):
            base = half * 2 * kw
            for r0 in range(0, kw, block):
                turns = jnp.dot(ref[r0 : r0 + block, :], spots, preferred_element_type=F32)
                r = turns - jnp.round(turns)
                zz = r * r
                s = r * horner(zz, SIN)
                co = horner(zz, COS)
                trig[base + r0 : base + r0 + block, columns] = (1.0 - s * s).astype(BF)
                trig[base + kw + r0 : base + kw + r0 + block, columns] = (s * co).astype(BF)

    step = min(2 * kw, 512)
    def part_sum(h, g, r0):
        columns = slice(g * group_cols, (g + 1) * group_cols)
        feats_g = feat_all[h, g * flat : (g + 1) * flat].reshape(group_cols, wc)
        return jnp.dot(trig[r0 : r0 + step, columns], feats_g, preferred_element_type=F32)

    def sums(h, g):
        for k in range(g * flat + (g != 1), (g + 1) * flat):
            if g == 1 or (g and k % flat):
                f_copies[h, k].wait_recv()
        swaps = []
        for r0 in range(0, 4 * kw, step):
            part = part_sum(h, g, r0)
            if g:
                part = factors[h, r0 : r0 + step, :] + part
            factors[h, r0 : r0 + step, :] = part
            if g == planes - 1:
                factors_out[h, r0 : r0 + step, :] = part.astype(BF)
                if (r0 + step) % (2 * kw) == 0:
                    half = r0 // (2 * kw)
                    swaps += [
                        core_copy(
                            factors_out.at[h, pl.ds(half_k * 2 * kw, 2 * kw)],
                            factors_in.at[h, pl.ds((1 - half_k) * 2 * kw, 2 * kw)],
                            2 + 2 * h + half_k,
                        )
                        for half_k in (half,)
                    ]
        return swaps

    scale = 1.0 / math.sqrt(atoms_all)

    def fields(h, swaps):
        for half, ref in enumerate((filt_ref, filt_other)):
            swaps[1 - half].wait_recv()
            filt = ref[:, h * wc : (h + 1) * wc].astype(F32) * scale
            for part in range(2):
                r0 = (2 * half + part) * kw
                total = factors[h, r0 : r0 + kw, :] + factors_in[h, r0 : r0 + kw, :].astype(F32)
                field_t[h, :, r0 : r0 + kw] = (total * filt).astype(BF).T

    inv_k = 1.0 / math.sqrt(kwaves_all)
    pair = 2

    def start_u(h, i, peer):
        u_copies[h, i] = remote(
            send_u.at[h, i], recv_u.at[h, i], u_send.at[h, i], u_recv.at[h, i], peer
        )

    def received(h, i):
        u_copies[h, i].wait_recv()
        return recv_u[h, i].astype(F32)

    def update(h, i):
        both = jnp.dot(
            field_t[h], trig[:, i * rows : (i + pair) * rows], preferred_element_type=F32
        )
        for k in range(i, i + pair):
            dz, dc, db = k // flat, k // side % side, k % side
            block_k = both[:, (k - i) * rows : (k - i + 1) * rows]
            if dz == 1 or (dz and (db or dc)):
                send_u[h, k] = block_k.astype(BF)
                start_u(h, k, back(1, 0, 0) if dz == 1 else back(0, db, dc))
            else:
                kept[h, flat + dz if dz else k] = block_k

    def push(h):
        for k in (*range(2 * flat, 3 * flat, pair), *range(1 * flat, 2 * flat, pair), *range(3 * flat, n, pair), *range(0 * flat, 1 * flat, pair)):
            update(h, k)

    def edges_out(h):
        for db, dc in near:
            i = ident(0, db, dc)
            acc = kept[h, i] + received(h, flat + i)
            send_u[h, i] = acc.astype(BF)
            start_u(h, i, back(0, db, dc))

    def columns_out(h, planes_out):
        for dz in planes_out:
            acc = kept[h, flat + dz]
            for db, dc in near:
                acc = acc + received(h, ident(dz, db, dc))
            send_u[h, dz * flat] = acc.astype(BF)
            start_u(h, dz * flat, back(dz, 0, 0))

    def mine(h):
        acc = kept[h, 0] + received(h, flat)
        for db, dc in near:
            acc = acc + received(h, ident(0, db, dc))
        for dz in far:
            acc = acc + received(h, dz * flat)
        return acc

    for h in range(1, parts):
        begin(h)
    angles(0, 1)
    p_forward()
    for h in range(parts):
        for dz in far:
            spread(h, dz)
            if dz == 2:
                across(h)
    angles(1, 1)
    for k in range(pair, n, pair):
        angles(k, pair)
    for copy in local[4:]:
        copy.wait()
    filt_copy.wait_recv()
    for h in range(parts):
        for g in range(planes):
            swaps = sums(h, g)
        fields(h, swaps)
        push(h)
    for h in range(parts):
        columns_out(h, far[:1])
        edges_out(h)
        columns_out(h, far[1:])
    gathered = jnp.concatenate([mine(h) for h in range(parts)], axis=0)
    mixed = jnp.dot(gathered.T, mixing_ref[...], precision=HIGHEST, preferred_element_type=F32)

    state = feats + mixed * inv_k
    meansq = jnp.mean(state * state, axis=1, keepdims=True)
    normed = (state * lax.rsqrt(meansq + 1e-06) * gain_ref[...].reshape(1, width)).astype(BF)
    inner = jnp.dot(normed, w_in_ref[...], preferred_element_type=F32)
    hidden = (inner / (1.0 + jnp.exp(-inner))).astype(BF)
    result = state + jnp.dot(hidden, w_out_ref[...], preferred_element_type=F32)
    out_ref[...] = jnp.where(live, result, 0.0)

    for copy in sent:
        copy.wait_send()


def body(n, cores, positions, counts, feats, waves, wave_filter, mixing, gain, w_in, w_out):
    rows, width = feats.shape
    planes, side = grid_of(n)
    kwaves_all = waves.shape[1] * cores
    kw = waves.shape[1] // n
    wc = width // PARTS
    vmem = pl.BlockSpec(memory_space=pltpu.VMEM)
    hbm = pl.BlockSpec(memory_space=pltpu.HBM)
    held = [
        pltpu.with_memory_space_constraint(array, pltpu.HBM)
        for array in (positions, feats, waves, wave_filter, mixing, gain, w_in, w_out)
    ]
    return pl.pallas_call(
        functools.partial(kernel, n, planes, side, rows * n * cores, kwaves_all),
        out_shape=pltpu.VMEM((rows, width), F32),
        in_specs=[pl.BlockSpec(memory_space=pltpu.SMEM)]
        + [hbm] * 8,
        out_specs=vmem,
        scratch_shapes=[
            pltpu.VMEM(positions.shape, F32),
            pltpu.VMEM(feats.shape, BF),
            pltpu.VMEM((3, max(kw, 128)), waves.dtype),
            pltpu.VMEM(gain.shape, F32),
            pltpu.VMEM((kw, width), BF),
            pltpu.VMEM((kw, width), BF),
            pltpu.VMEM(mixing.shape, F32),
            pltpu.VMEM(w_in.shape, BF),
            pltpu.VMEM(w_out.shape, BF),
            pltpu.VMEM((16, max(kw, 128)), F32),
            pltpu.VMEM((kw, 16), BF),
            pltpu.VMEM((3, max(kw, 128)), waves.dtype),
            pltpu.VMEM((n, 16, rows), BF),
            pltpu.VMEM((PARTS, n, rows, wc), BF),
            pltpu.VMEM((kw, 16), BF),
            pltpu.VMEM((4 * kw, n * rows), BF),
            pltpu.VMEM((PARTS, 4 * kw, wc), F32),
            pltpu.VMEM((PARTS, 4 * kw, wc), BF),
            pltpu.VMEM((PARTS, 4 * kw, wc), BF),
            pltpu.VMEM((PARTS, wc, 4 * kw), BF),
            pltpu.VMEM((PARTS, planes + side * side, wc, rows), F32),
            pltpu.VMEM((PARTS, n, wc, rows), BF),
            pltpu.VMEM((PARTS, n, wc, rows), BF),
        ]
        + [pltpu.SemaphoreType.DMA((n,))] * 2
        + [pltpu.SemaphoreType.DMA((PARTS, n))] * 4
        + [pltpu.SemaphoreType.DMA((2 + 2 * PARTS,))] * 2
        + [pltpu.SemaphoreType.DMA((8,))],
        compiler_params=pltpu.CompilerParams(
            collective_id=0, has_side_effects=True, vmem_limit_bytes=48 * 2**20
        ),
    )(counts, *held).astype(BF)


def solution(mesh):
    n, cores = mesh.shape["atom"], mesh.shape["wave"]
    return jax.shard_map(
        functools.partial(body, n, cores),
        mesh=mesh,
        in_specs=(
            P(None, ("atom", "wave")),
            P(("atom", "wave")),
            P(("atom", "wave"), None),
            P(None, "wave"),
            P("wave", None),
            P(),
            P(),
            P(),
            P(),
        ),
        out_specs=P(("atom", "wave"), None),
        check_vma=False,
    )
```

```python
import functools
import math

import jax
import jax.numpy as jnp
from jax import lax
from jax.experimental import pallas as pl
from jax.experimental.pallas import tpu as pltpu
from jax.sharding import PartitionSpec as P

MESH = pl.DeviceIdType.MESH
BF, F32 = jnp.bfloat16, jnp.float32
HIGHEST = lax.Precision.HIGHEST
SIN = (4.442879586450294, -7.307818046861918, 3.5977887167859492, -0.7912381728222249)
COS = (1.414204080391997, -6.977642051264664, 5.715238335828671, -1.7283485048567975)
PARTS = 1


def horner(z, coefs):
    total = coefs[-1]
    for value in coefs[-2::-1]:
        total = total * z + value
    return total


def grid_of(n):
    side = 1
    while n % (4 * side * side) == 0 and 8 * side**3 <= n:
        side *= 2
    return n // (side * side), side


def kernel(
    n,
    planes,
    side,
    atoms_all,
    kwaves_all,
    counts_ref,
    pos_hbm,
    feats_hbm,
    waves_hbm,
    filt_hbm,
    mixing_hbm,
    gain_hbm,
    w_in_hbm,
    w_out_hbm,
    out_ref,
    pos_ref,
    feats_ref,
    waves_ref,
    gain_ref,
    filt_ref,
    filt_other,
    mixing_ref,
    w_in_ref,
    w_out_ref,
    stage,
    wave_own,
    wave_raw,
    pos_all,
    feat_all,
    wave_other,
    trig,
    factors,
    factors_out,
    factors_in,
    field_t,
    kept,
    send_u,
    recv_u,
    p_send,
    p_recv,
    f_send,
    f_recv,
    u_send,
    u_recv,
    c_send,
    c_recv,
    l_sem,
):
    kw, width = filt_ref.shape
    rows = feats_ref.shape[0]
    parts = feat_all.shape[0]
    wc = width // parts
    me = lax.axis_index("atom")
    core = lax.axis_index("wave")
    x = me % side
    y = (me // side) % side
    z = me // (side * side)
    b = y + core * (x - y)
    c = x + core * (y - x)
    stride_b = side + core * (1 - side)
    stride_c = 1 + core * (side - 1)

    def ident(dz, db, dc):
        return (dz * side + dc) * side + db

    def crossed(value, mask):
        bit = 1
        while bit <= mask:
            if mask & bit:
                value = value + bit * (1 - 2 * ((value // bit) % 2))
            bit *= 2
        return value

    def ahead(dz, db, dc):
        zz, bb, cc = crossed(z, dz), (b + db) % side, (c + dc) % side
        return (zz * (side * side) + bb * stride_b + cc * stride_c, core)

    def back(dz, db, dc):
        return ahead(dz, side - db, side - dc)

    partner = (me, 1 - core)
    far = range(2, planes)
    near = [(db, dc) for dc in range(side) for db in range(side) if db or dc]
    every = [(dz, db, dc) for dz in range(planes) for dc in range(side) for db in range(side)][1:]
    flat = side * side

    barrier = pltpu.get_barrier_semaphore()
    peers = [partner] + [ahead(dz, 0, 0) for dz in range(1, planes)]
    peers += [ahead(0, db, dc) for db, dc in near]
    for peer in peers:
        pl.semaphore_signal(barrier, inc=1, device_id=peer, device_id_type=MESH)

    window = max(kw, 128)
    first = pl.multiple_of((me * kw) // window * window, window)
    shift = me * kw - first
    local = [
        pltpu.make_async_copy(src, dst, l_sem.at[k])
        for k, (src, dst) in enumerate(
            (
                (feats_hbm, feats_ref),
                (pos_hbm, pos_ref),
                (waves_hbm.at[:, pl.ds(first, window)], waves_ref),
                (filt_hbm.at[pl.ds(pl.multiple_of(me * kw, kw), kw)], filt_ref),
                (mixing_hbm, mixing_ref),
                (w_in_hbm, w_in_ref),
                (w_out_hbm, w_out_ref),
                (gain_hbm, gain_ref),
            )
        )
    ]
    for copy in local[:3]:
        copy.start()

    local[0].wait()
    slot = lax.broadcasted_iota(jnp.int32, (rows, width), 0)
    live = slot < counts_ref[0]
    feats = feats_ref[...].astype(F32)
    masked = jnp.where(live, feats, 0.0).astype(BF)
    for h in range(parts):
        feat_all[h, 0] = masked[:, h * wc : (h + 1) * wc]
    local[1].wait()
    place = pos_ref[...]
    high = place.astype(BF).astype(F32)
    middle = (place - high).astype(BF).astype(F32)
    stage[...] = jnp.zeros_like(stage)
    stage[0:3, :rows] = high
    stage[3:6, :rows] = middle
    stage[6:9, :rows] = place - high - middle
    pos_all[0] = stage[:, :rows].astype(BF)

    def turned(raw):
        for part in range(3):
            stage[3 * part : 3 * part + 3, :] = raw.astype(F32)
        found = stage[...]
        if kw < window:
            found = pltpu.roll(found, (window - shift) % window, 1)
        return found.T[:kw].astype(BF)

    sent = []

    def remote(src, dst, send, recv, peer):
        copy = pltpu.make_async_remote_copy(
            src_ref=src,
            dst_ref=dst,
            send_sem=send,
            recv_sem=recv,
            device_id=peer,
            device_id_type=MESH,
        )
        copy.start()
        sent.append(copy)
        return copy

    f_copies, u_copies, p_copies = {}, {}, {}

    def send_place(src, dst, peer):
        p_copies[dst] = remote(
            pos_all.at[src], pos_all.at[dst], p_send.at[dst], p_recv.at[dst], peer
        )

    def p_begin():
        for dz in range(1, planes):
            send_place(0, dz * flat, ahead(dz, 0, 0))
        for db, dc in near:
            send_place(0, ident(0, db, dc), ahead(0, db, dc))

    def p_forward():
        for db, dc in near:
            i = ident(0, db, dc)
            p_copies[i].wait_recv()
            send_place(i, flat + i, ahead(1, 0, 0))
        for dz in far:
            p_copies[dz * flat].wait_recv()
            for db, dc in near:
                send_place(dz * flat, ident(dz, db, dc), ahead(0, db, dc))

    def send_feat(h, src, dst, peer):
        f_copies[h, dst] = remote(
            feat_all.at[h, src], feat_all.at[h, dst], f_send.at[h, dst], f_recv.at[h, dst], peer
        )

    def begin(h):
        spread(h, 0)
        for dz in (*far, 1):
            send_feat(h, 0, dz * flat, ahead(dz, 0, 0))

    def spread(h, dz):
        if dz:
            f_copies[h, dz * flat].wait_recv()
        for db, dc in near:
            send_feat(h, ident(dz, 0, 0), ident(dz, db, dc), ahead(0, db, dc))

    def across(h):
        for db, dc in near:
            f_copies[h, ident(0, db, dc)].wait_recv()
            send_feat(h, ident(0, db, dc), ident(1, db, dc), ahead(1, 0, 0))

    def core_copy(src, dst, k):
        return remote(src, dst, c_send.at[k], c_recv.at[k], partner)

    pl.semaphore_wait(barrier, len(peers))
    p_begin()
    begin(0)
    for copy in local[3:]:
        copy.start()
    local[2].wait()
    wave_copy = core_copy(waves_ref, wave_raw, 0)
    wave_own[...] = turned(waves_ref[...])
    local[3].wait()
    filt_copy = core_copy(filt_ref, filt_other, 1)
    wave_copy.wait_recv()
    wave_other[...] = turned(wave_raw[...])

    block = min(kw, 128)
    group_cols = flat * rows

    def angles(start, count):
        for k in range(start, start + count):
            if k == flat or (k > flat and k % flat):
                p_copies[k].wait_recv()
        columns = slice(start * rows, (start + count) * rows)
        spots = jnp.concatenate([pos_all[start + d] for d in range(count)], axis=1)
        for half, ref in enumerate((wave_own, wave_other)):
            base = half * 2 * kw
            for r0 in range(0, kw, block):
                turns = jnp.dot(ref[r0 : r0 + block, :], spots, preferred_element_type=F32)
                r = turns - ((turns + 12582912.0) - 12582912.0)
                zz = r * r
                s = r * horner(zz, SIN)
                co = horner(zz, COS)
                trig[base + r0 : base + r0 + block, columns] = (1.0 - s * s).astype(BF)
                trig[base + kw + r0 : base + kw + r0 + block, columns] = (s * co).astype(BF)

    step = min(2 * kw, 512)
    def part_sum(h, g, r0):
        columns = slice(g * group_cols, (g + 1) * group_cols)
        feats_g = feat_all[h, g * flat : (g + 1) * flat].reshape(group_cols, wc)
        return jnp.dot(trig[r0 : r0 + step, columns], feats_g, preferred_element_type=F32)

    def sums(h, g):
        for k in range(g * flat + (g != 1), (g + 1) * flat):
            if g == 1 or (g and k % flat):
                f_copies[h, k].wait_recv()
        swaps = []
        for r0 in range(0, 4 * kw, step):
            part = part_sum(h, g, r0)
            if g:
                part = factors[h, r0 : r0 + step, :] + part
            factors[h, r0 : r0 + step, :] = part
            if g == planes - 1:
                factors_out[h, r0 : r0 + step, :] = part.astype(BF)
                if r0 + step == 4 * kw:
                    swaps.append(core_copy(factors_out.at[h], factors_in.at[h], 2 + h))
        return swaps

    scale = 1.0 / math.sqrt(atoms_all)

    def fields(h, swaps):
        for half, ref in enumerate((filt_ref, filt_other)):
            if half == 0:
                swaps[0].wait_recv()
            filt = ref[:, h * wc : (h + 1) * wc].astype(F32) * scale
            for part in range(2):
                r0 = (2 * half + part) * kw
                total = factors[h, r0 : r0 + kw, :] + factors_in[h, (r0 + 2 * kw) % (4 * kw) : (r0 + 2 * kw) % (4 * kw) + kw, :].astype(F32)
                field_t[h, :, r0 : r0 + kw] = (total * filt).astype(BF).T

    inv_k = 1.0 / math.sqrt(kwaves_all)
    pair = 2

    def start_u(h, i, peer):
        u_copies[h, i] = remote(
            send_u.at[h, i], recv_u.at[h, i], u_send.at[h, i], u_recv.at[h, i], peer
        )

    def received(h, i):
        u_copies[h, i].wait_recv()
        return recv_u[h, i].astype(F32)

    def update(h, i):
        both = jnp.dot(
            field_t[h], trig[:, i * rows : (i + pair) * rows], preferred_element_type=F32
        )
        for k in range(i, i + pair):
            dz, dc, db = k // flat, k // side % side, k % side
            block_k = both[:, (k - i) * rows : (k - i + 1) * rows]
            if dz == 1 or (dz and (db or dc)):
                send_u[h, k] = block_k.astype(BF)
                start_u(h, k, back(1, 0, 0) if dz == 1 else back(0, db, dc))
            else:
                kept[h, flat + dz if dz else k] = block_k

    def push(h):
        for k in (*range(2 * flat, 3 * flat, pair), *range(1 * flat, 2 * flat, pair), *range(3 * flat, n, pair), *range(0 * flat, 1 * flat, pair)):
            update(h, k)

    def edges_out(h):
        for db, dc in near:
            i = ident(0, db, dc)
            acc = kept[h, i] + received(h, flat + i)
            send_u[h, i] = acc.astype(BF)
            start_u(h, i, back(0, db, dc))

    def columns_out(h, planes_out):
        for dz in planes_out:
            acc = kept[h, flat + dz]
            for db, dc in near:
                acc = acc + received(h, ident(dz, db, dc))
            send_u[h, dz * flat] = acc.astype(BF)
            start_u(h, dz * flat, back(dz, 0, 0))

    def mine(h):
        acc = kept[h, 0] + received(h, flat)
        for db, dc in near:
            acc = acc + received(h, ident(0, db, dc))
        for dz in far:
            acc = acc + received(h, dz * flat)
        return acc

    for h in range(1, parts):
        begin(h)
    angles(0, 1)
    p_forward()
    for h in range(parts):
        for dz in far:
            spread(h, dz)
            if dz == 2:
                across(h)
    angles(1, 1)
    for k in range(pair, n, pair):
        angles(k, pair)
    for copy in local[4:]:
        copy.wait()
    filt_copy.wait_recv()
    for h in range(parts):
        for g in range(planes):
            swaps = sums(h, g)
        fields(h, swaps)
        push(h)
    for h in range(parts):
        columns_out(h, far[:1])
        edges_out(h)
        columns_out(h, far[1:])
    gathered = jnp.concatenate([mine(h) for h in range(parts)], axis=0)
    mixed = jnp.dot(gathered.T, mixing_ref[...], precision=HIGHEST, preferred_element_type=F32)

    state = feats + mixed * inv_k
    meansq = jnp.mean(state * state, axis=1, keepdims=True)
    normed = (state * lax.rsqrt(meansq + 1e-06) * gain_ref[...].reshape(1, width)).astype(BF)
    inner = jnp.dot(normed, w_in_ref[...], preferred_element_type=F32)
    hidden = (inner / (1.0 + jnp.exp(-inner))).astype(BF)
    result = state + jnp.dot(hidden, w_out_ref[...], preferred_element_type=F32)
    out_ref[...] = jnp.where(live, result, 0.0)

    for copy in sent:
        copy.wait_send()


def body(n, cores, positions, counts, feats, waves, wave_filter, mixing, gain, w_in, w_out):
    rows, width = feats.shape
    planes, side = grid_of(n)
    kwaves_all = waves.shape[1] * cores
    kw = waves.shape[1] // n
    wc = width // PARTS
    vmem = pl.BlockSpec(memory_space=pltpu.VMEM)
    hbm = pl.BlockSpec(memory_space=pltpu.HBM)
    held = [
        pltpu.with_memory_space_constraint(array, pltpu.HBM)
        for array in (positions, feats, waves, wave_filter, mixing, gain, w_in, w_out)
    ]
    return pl.pallas_call(
        functools.partial(kernel, n, planes, side, rows * n * cores, kwaves_all),
        out_shape=pltpu.VMEM((rows, width), F32),
        in_specs=[pl.BlockSpec(memory_space=pltpu.SMEM)]
        + [hbm] * 8,
        out_specs=vmem,
        scratch_shapes=[
            pltpu.VMEM(positions.shape, F32),
            pltpu.VMEM(feats.shape, BF),
            pltpu.VMEM((3, max(kw, 128)), waves.dtype),
            pltpu.VMEM(gain.shape, F32),
            pltpu.VMEM((kw, width), BF),
            pltpu.VMEM((kw, width), BF),
            pltpu.VMEM(mixing.shape, F32),
            pltpu.VMEM(w_in.shape, BF),
            pltpu.VMEM(w_out.shape, BF),
            pltpu.VMEM((16, max(kw, 128)), F32),
            pltpu.VMEM((kw, 16), BF),
            pltpu.VMEM((3, max(kw, 128)), waves.dtype),
            pltpu.VMEM((n, 16, rows), BF),
            pltpu.VMEM((PARTS, n, rows, wc), BF),
            pltpu.VMEM((kw, 16), BF),
            pltpu.VMEM((4 * kw, n * rows), BF),
            pltpu.VMEM((PARTS, 4 * kw, wc), F32),
            pltpu.VMEM((PARTS, 4 * kw, wc), BF),
            pltpu.VMEM((PARTS, 4 * kw, wc), BF),
            pltpu.VMEM((PARTS, wc, 4 * kw), BF),
            pltpu.VMEM((PARTS, planes + side * side, wc, rows), F32),
            pltpu.VMEM((PARTS, n, wc, rows), BF),
            pltpu.VMEM((PARTS, n, wc, rows), BF),
        ]
        + [pltpu.SemaphoreType.DMA((n,))] * 2
        + [pltpu.SemaphoreType.DMA((PARTS, n))] * 4
        + [pltpu.SemaphoreType.DMA((2 + 2 * PARTS,))] * 2
        + [pltpu.SemaphoreType.DMA((8,))],
        compiler_params=pltpu.CompilerParams(
            collective_id=0, has_side_effects=True, vmem_limit_bytes=48 * 2**20
        ),
    )(counts, *held).astype(BF)


def solution(mesh):
    n, cores = mesh.shape["atom"], mesh.shape["wave"]
    return jax.shard_map(
        functools.partial(body, n, cores),
        mesh=mesh,
        in_specs=(
            P(None, ("atom", "wave")),
            P(("atom", "wave")),
            P(("atom", "wave"), None),
            P(None, "wave"),
            P("wave", None),
            P(),
            P(),
            P(),
            P(),
        ),
        out_specs=P(("atom", "wave"), None),
        check_vma=False,
    )
```

```python
import functools
import math

import jax
import jax.numpy as jnp
from jax import lax
from jax.experimental import pallas as pl
from jax.experimental.pallas import tpu as pltpu
from jax.sharding import PartitionSpec as P

MESH = pl.DeviceIdType.MESH
BF, F32 = jnp.bfloat16, jnp.float32
HIGHEST = lax.Precision.HIGHEST
SIN = (4.442879586450294, -7.307818046861918, 3.5977887167859492, -0.7912381728222249)
COS = (1.414204080391997, -6.977642051264664, 5.715238335828671, -1.7283485048567975)
PARTS = 1


def horner(z, coefs):
    total = coefs[-1]
    for value in coefs[-2::-1]:
        total = total * z + value
    return total


def grid_of(n):
    side = 1
    while n % (4 * side * side) == 0 and 8 * side**3 <= n:
        side *= 2
    return n // (side * side), side


def kernel(
    n,
    planes,
    side,
    atoms_all,
    kwaves_all,
    counts_ref,
    pos_hbm,
    feats_hbm,
    waves_hbm,
    filt_hbm,
    mixing_hbm,
    gain_hbm,
    w_in_hbm,
    w_out_hbm,
    out_ref,
    pos_ref,
    feats_ref,
    waves_ref,
    gain_ref,
    filt_ref,
    filt_other,
    mixing_ref,
    w_in_ref,
    w_out_ref,
    stage,
    wave_own,
    wave_raw,
    pos_all,
    feat_all,
    wave_other,
    trig,
    factors,
    factors_out,
    factors_in,
    field_t,
    kept,
    send_u,
    recv_u,
    p_send,
    p_recv,
    f_send,
    f_recv,
    u_send,
    u_recv,
    c_send,
    c_recv,
    l_sem,
):
    kw, width = filt_ref.shape
    rows = feats_ref.shape[0]
    parts = feat_all.shape[0]
    wc = width // parts
    me = lax.axis_index("atom")
    core = lax.axis_index("wave")
    x = me % side
    y = (me // side) % side
    z = me // (side * side)
    b = y + core * (x - y)
    c = x + core * (y - x)
    stride_b = side + core * (1 - side)
    stride_c = 1 + core * (side - 1)

    def ident(dz, db, dc):
        return (dz * side + dc) * side + db

    def crossed(value, mask):
        bit = 1
        while bit <= mask:
            if mask & bit:
                value = value + bit * (1 - 2 * ((value // bit) % 2))
            bit *= 2
        return value

    def ahead(dz, db, dc):
        zz, bb, cc = crossed(z, dz), (b + db) % side, (c + dc) % side
        return (zz * (side * side) + bb * stride_b + cc * stride_c, core)

    def back(dz, db, dc):
        return ahead(dz, side - db, side - dc)

    partner = (me, 1 - core)
    far = range(2, planes)
    near = [(db, dc) for dc in range(side) for db in range(side) if db or dc]
    every = [(dz, db, dc) for dz in range(planes) for dc in range(side) for db in range(side)][1:]
    flat = side * side

    barrier = pltpu.get_barrier_semaphore()
    peers = [partner] + [ahead(dz, 0, 0) for dz in range(1, planes)]
    peers += [ahead(0, db, dc) for db, dc in near]
    for peer in peers:
        pl.semaphore_signal(barrier, inc=1, device_id=peer, device_id_type=MESH)

    window = max(kw, 128)
    first = pl.multiple_of((me * kw) // window * window, window)
    shift = me * kw - first
    local = [
        pltpu.make_async_copy(src, dst, l_sem.at[k])
        for k, (src, dst) in enumerate(
            (
                (feats_hbm, feats_ref),
                (pos_hbm, pos_ref),
                (waves_hbm.at[:, pl.ds(first, window)], waves_ref),
                (filt_hbm.at[pl.ds(pl.multiple_of(me * kw, kw), kw)], filt_ref),
                (mixing_hbm, mixing_ref),
                (w_in_hbm, w_in_ref),
                (w_out_hbm, w_out_ref),
                (gain_hbm, gain_ref),
            )
        )
    ]
    for copy in local[:3]:
        copy.start()

    local[0].wait()
    slot = lax.broadcasted_iota(jnp.int32, (rows, width), 0)
    live = slot < counts_ref[0]
    feats = feats_ref[...].astype(F32)
    masked = jnp.where(live, feats, 0.0).astype(BF)
    for h in range(parts):
        feat_all[h, 0] = masked[:, h * wc : (h + 1) * wc]
    local[1].wait()
    place = pos_ref[...]
    high = place.astype(BF).astype(F32)
    middle = (place - high).astype(BF).astype(F32)
    stage[...] = jnp.zeros_like(stage)
    stage[0:3, :rows] = high
    stage[3:6, :rows] = middle
    stage[6:9, :rows] = place - high - middle
    pos_all[0] = stage[:, :rows].astype(BF)

    def turned(raw):
        for part in range(3):
            stage[3 * part : 3 * part + 3, :] = raw.astype(F32)
        found = stage[...]
        if kw < window:
            found = pltpu.roll(found, (window - shift) % window, 1)
        return found.T[:kw].astype(BF)

    sent = []

    def remote(src, dst, send, recv, peer):
        copy = pltpu.make_async_remote_copy(
            src_ref=src,
            dst_ref=dst,
            send_sem=send,
            recv_sem=recv,
            device_id=peer,
            device_id_type=MESH,
        )
        copy.start()
        sent.append(copy)
        return copy

    f_copies, u_copies, p_copies = {}, {}, {}

    def send_place(src, dst, peer):
        p_copies[dst] = remote(
            pos_all.at[src], pos_all.at[dst], p_send.at[dst], p_recv.at[dst], peer
        )

    def p_begin():
        for dz in range(1, planes):
            send_place(0, dz * flat, ahead(dz, 0, 0))
        for db, dc in near:
            send_place(0, ident(0, db, dc), ahead(0, db, dc))

    def p_forward():
        for db, dc in near:
            i = ident(0, db, dc)
            p_copies[i].wait_recv()
            send_place(i, flat + i, ahead(1, 0, 0))
        for dz in far:
            p_copies[dz * flat].wait_recv()
            for db, dc in near:
                send_place(dz * flat, ident(dz, db, dc), ahead(0, db, dc))

    def send_feat(h, src, dst, peer):
        f_copies[h, dst] = remote(
            feat_all.at[h, src], feat_all.at[h, dst], f_send.at[h, dst], f_recv.at[h, dst], peer
        )

    def begin(h):
        spread(h, 0)
        for dz in (*far, 1):
            send_feat(h, 0, dz * flat, ahead(dz, 0, 0))

    def spread(h, dz):
        if dz:
            f_copies[h, dz * flat].wait_recv()
        for db, dc in near:
            send_feat(h, ident(dz, 0, 0), ident(dz, db, dc), ahead(0, db, dc))

    def across(h):
        for db, dc in near:
            f_copies[h, ident(0, db, dc)].wait_recv()
            send_feat(h, ident(0, db, dc), ident(1, db, dc), ahead(1, 0, 0))

    def core_copy(src, dst, k):
        return remote(src, dst, c_send.at[k], c_recv.at[k], partner)

    pl.semaphore_wait(barrier, len(peers))
    p_begin()
    begin(0)
    for copy in local[3:]:
        copy.start()
    local[2].wait()
    wave_copy = core_copy(waves_ref, wave_raw, 0)
    wave_own[...] = turned(waves_ref[...])
    local[3].wait()
    filt_copy = core_copy(filt_ref, filt_other, 1)
    wave_copy.wait_recv()
    wave_other[...] = turned(wave_raw[...])

    block = min(kw, 128)
    group_cols = flat * rows

    def angles(start, count):
        for k in range(start, start + count):
            if k == flat or (k > flat and k % flat):
                p_copies[k].wait_recv()
        columns = slice(start * rows, (start + count) * rows)
        spots = jnp.concatenate([pos_all[start + d] for d in range(count)], axis=1)
        for half, ref in enumerate((wave_own, wave_other)):
            base = half * 2 * kw
            for r0 in range(0, kw, block):
                turns = jnp.dot(ref[r0 : r0 + block, :], spots, preferred_element_type=F32)
                r = turns - ((turns + 12582912.0) - 12582912.0)
                zz = r * r
                s = r * horner(zz, SIN)
                co = horner(zz, COS)
                trig[base + r0 : base + r0 + block, columns] = (1.0 - s * s).astype(BF)
                trig[base + kw + r0 : base + kw + r0 + block, columns] = (s * co).astype(BF)

    step = min(2 * kw, 512)
    def part_sum(h, start, count, r0):
        columns = slice(start * rows, (start + count) * rows)
        spots = feat_all[h, start : start + count].reshape(count * rows, wc)
        return jnp.dot(trig[r0 : r0 + step, columns], spots, preferred_element_type=F32)

    def sums(h, start, count):
        for k in range(start, start + count):
            if k >= flat and (k % flat or k == flat):
                f_copies[h, k].wait_recv()
        swaps = []
        for r0 in range(0, 4 * kw, step):
            part = part_sum(h, start, count, r0)
            if start:
                part = factors[h, r0 : r0 + step, :] + part
            if start + count < n:
                factors[h, r0 : r0 + step, :] = part
            else:
                factors[h, r0 : r0 + step, :] = part
                factors_out[h, r0 : r0 + step, :] = part.astype(BF)
                if r0 + step == 4 * kw:
                    swaps.append(core_copy(factors_out.at[h], factors_in.at[h], 2 + h))
        return swaps

    scale = 1.0 / math.sqrt(atoms_all)

    def fields(h, swaps):
        for half, ref in enumerate((filt_ref, filt_other)):
            if half == 0:
                swaps[0].wait_recv()
            filt = ref[:, h * wc : (h + 1) * wc].astype(F32) * scale
            for part in range(2):
                r0 = (2 * half + part) * kw
                total = factors[h, r0 : r0 + kw, :] + factors_in[h, (r0 + 2 * kw) % (4 * kw) : (r0 + 2 * kw) % (4 * kw) + kw, :].astype(F32)
                field_t[h, :, r0 : r0 + kw] = (total * filt).astype(BF).T

    inv_k = 1.0 / math.sqrt(kwaves_all)
    pair = 2

    def start_u(h, i, peer):
        u_copies[h, i] = remote(
            send_u.at[h, i], recv_u.at[h, i], u_send.at[h, i], u_recv.at[h, i], peer
        )

    def received(h, i):
        u_copies[h, i].wait_recv()
        return recv_u[h, i].astype(F32)

    def update(h, i):
        both = jnp.dot(
            field_t[h], trig[:, i * rows : (i + pair) * rows], preferred_element_type=F32
        )
        for k in range(i, i + pair):
            dz, dc, db = k // flat, k // side % side, k % side
            block_k = both[:, (k - i) * rows : (k - i + 1) * rows]
            if dz == 1 or (dz and (db or dc)):
                send_u[h, k] = block_k.astype(BF)
                start_u(h, k, back(1, 0, 0) if dz == 1 else back(0, db, dc))
            else:
                kept[h, flat + dz if dz else k] = block_k

    def push(h):
        for k in (*range(2 * flat, 3 * flat, pair), *range(1 * flat, 2 * flat, pair), *range(3 * flat, n, pair), *range(0 * flat, 1 * flat, pair)):
            update(h, k)

    def edges_out(h):
        for db, dc in near:
            i = ident(0, db, dc)
            acc = kept[h, i] + received(h, flat + i)
            send_u[h, i] = acc.astype(BF)
            start_u(h, i, back(0, db, dc))

    def columns_out(h, planes_out):
        for dz in planes_out:
            acc = kept[h, flat + dz]
            for db, dc in near:
                acc = acc + received(h, ident(dz, db, dc))
            send_u[h, dz * flat] = acc.astype(BF)
            start_u(h, dz * flat, back(dz, 0, 0))

    def mine(h):
        acc = kept[h, 0] + received(h, flat)
        for db, dc in near:
            acc = acc + received(h, ident(0, db, dc))
        for dz in far:
            acc = acc + received(h, dz * flat)
        return acc

    for h in range(1, parts):
        begin(h)
    angles(0, 1)
    p_forward()
    for h in range(parts):
        for dz in far:
            spread(h, dz)
            if dz == 2:
                across(h)
    angles(1, 1)
    for k in range(pair, n, pair):
        angles(k, pair)
    for copy in local[4:]:
        copy.wait()
    filt_copy.wait_recv()
    for h in range(parts):
        for k in range(0, n, flat // 2):
            swaps = sums(h, k, flat // 2)
        fields(h, swaps)
        push(h)
    for h in range(parts):
        columns_out(h, far[:1])
        edges_out(h)
        columns_out(h, far[1:])
    gathered = jnp.concatenate([mine(h) for h in range(parts)], axis=0)
    mixed = jnp.dot(gathered.T, mixing_ref[...], precision=HIGHEST, preferred_element_type=F32)

    state = feats + mixed * inv_k
    meansq = jnp.mean(state * state, axis=1, keepdims=True)
    normed = (state * lax.rsqrt(meansq + 1e-06) * gain_ref[...].reshape(1, width)).astype(BF)
    inner = jnp.dot(normed, w_in_ref[...], preferred_element_type=F32)
    hidden = (inner / (1.0 + jnp.exp(-inner))).astype(BF)
    result = state + jnp.dot(hidden, w_out_ref[...], preferred_element_type=F32)
    out_ref[...] = jnp.where(live, result, 0.0)

    for copy in sent:
        copy.wait_send()


def body(n, cores, positions, counts, feats, waves, wave_filter, mixing, gain, w_in, w_out):
    rows, width = feats.shape
    planes, side = grid_of(n)
    kwaves_all = waves.shape[1] * cores
    kw = waves.shape[1] // n
    wc = width // PARTS
    vmem = pl.BlockSpec(memory_space=pltpu.VMEM)
    hbm = pl.BlockSpec(memory_space=pltpu.HBM)
    held = [
        pltpu.with_memory_space_constraint(array, pltpu.HBM)
        for array in (positions, feats, waves, wave_filter, mixing, gain, w_in, w_out)
    ]
    return pl.pallas_call(
        functools.partial(kernel, n, planes, side, rows * n * cores, kwaves_all),
        out_shape=pltpu.VMEM((rows, width), F32),
        in_specs=[pl.BlockSpec(memory_space=pltpu.SMEM)]
        + [hbm] * 8,
        out_specs=vmem,
        scratch_shapes=[
            pltpu.VMEM(positions.shape, F32),
            pltpu.VMEM(feats.shape, BF),
            pltpu.VMEM((3, max(kw, 128)), waves.dtype),
            pltpu.VMEM(gain.shape, F32),
            pltpu.VMEM((kw, width), BF),
            pltpu.VMEM((kw, width), BF),
            pltpu.VMEM(mixing.shape, F32),
            pltpu.VMEM(w_in.shape, BF),
            pltpu.VMEM(w_out.shape, BF),
            pltpu.VMEM((16, max(kw, 128)), F32),
            pltpu.VMEM((kw, 16), BF),
            pltpu.VMEM((3, max(kw, 128)), waves.dtype),
            pltpu.VMEM((n, 16, rows), BF),
            pltpu.VMEM((PARTS, n, rows, wc), BF),
            pltpu.VMEM((kw, 16), BF),
            pltpu.VMEM((4 * kw, n * rows), BF),
            pltpu.VMEM((PARTS, 4 * kw, wc), F32),
            pltpu.VMEM((PARTS, 4 * kw, wc), BF),
            pltpu.VMEM((PARTS, 4 * kw, wc), BF),
            pltpu.VMEM((PARTS, wc, 4 * kw), BF),
            pltpu.VMEM((PARTS, planes + side * side, wc, rows), F32),
            pltpu.VMEM((PARTS, n, wc, rows), BF),
            pltpu.VMEM((PARTS, n, wc, rows), BF),
        ]
        + [pltpu.SemaphoreType.DMA((n,))] * 2
        + [pltpu.SemaphoreType.DMA((PARTS, n))] * 4
        + [pltpu.SemaphoreType.DMA((2 + 2 * PARTS,))] * 2
        + [pltpu.SemaphoreType.DMA((8,))],
        compiler_params=pltpu.CompilerParams(
            collective_id=0, has_side_effects=True, vmem_limit_bytes=48 * 2**20
        ),
    )(counts, *held).astype(BF)


def solution(mesh):
    n, cores = mesh.shape["atom"], mesh.shape["wave"]
    return jax.shard_map(
        functools.partial(body, n, cores),
        mesh=mesh,
        in_specs=(
            P(None, ("atom", "wave")),
            P(("atom", "wave")),
            P(("atom", "wave"), None),
            P(None, "wave"),
            P("wave", None),
            P(),
            P(),
            P(),
            P(),
        ),
        out_specs=P(("atom", "wave"), None),
        check_vma=False,
    )
```

```python
import functools
import math

import jax
import jax.numpy as jnp
from jax import lax
from jax.experimental import pallas as pl
from jax.experimental.pallas import tpu as pltpu
from jax.sharding import PartitionSpec as P

MESH = pl.DeviceIdType.MESH
BF, F32 = jnp.bfloat16, jnp.float32
HIGHEST = lax.Precision.HIGHEST
SIN = (4.442879586450294, -7.307818046861918, 3.5977887167859492, -0.7912381728222249)
COS = (1.414204080391997, -6.977642051264664, 5.715238335828671, -1.7283485048567975)
PARTS = 1


def horner(z, coefs):
    total = coefs[-1]
    for value in coefs[-2::-1]:
        total = total * z + value
    return total


def grid_of(n):
    side = 1
    while n % (4 * side * side) == 0 and 8 * side**3 <= n:
        side *= 2
    return n // (side * side), side


def kernel(
    n,
    planes,
    side,
    atoms_all,
    kwaves_all,
    counts_ref,
    pos_hbm,
    feats_hbm,
    waves_hbm,
    filt_hbm,
    mixing_hbm,
    gain_hbm,
    w_in_hbm,
    w_out_hbm,
    out_ref,
    pos_ref,
    feats_ref,
    waves_ref,
    gain_ref,
    filt_ref,
    filt_other,
    mixing_ref,
    w_in_ref,
    w_out_ref,
    stage,
    wave_own,
    wave_raw,
    pos_all,
    feat_all,
    wave_other,
    trig,
    factors,
    factors_out,
    factors_in,
    field_t,
    kept,
    send_u,
    recv_u,
    p_send,
    p_recv,
    f_send,
    f_recv,
    u_send,
    u_recv,
    c_send,
    c_recv,
    l_sem,
):
    kw, width = filt_ref.shape
    rows = feats_ref.shape[0]
    parts = feat_all.shape[0]
    wc = width // parts
    me = lax.axis_index("atom")
    core = lax.axis_index("wave")
    x = me % side
    y = (me // side) % side
    z = me // (side * side)
    b = y + core * (x - y)
    c = x + core * (y - x)
    stride_b = side + core * (1 - side)
    stride_c = 1 + core * (side - 1)

    def ident(dz, db, dc):
        return (dz * side + dc) * side + db

    def crossed(value, mask):
        bit = 1
        while bit <= mask:
            if mask & bit:
                value = value + bit * (1 - 2 * ((value // bit) % 2))
            bit *= 2
        return value

    def ahead(dz, db, dc):
        zz, bb, cc = crossed(z, dz), (b + db) % side, (c + dc) % side
        return (zz * (side * side) + bb * stride_b + cc * stride_c, core)

    def back(dz, db, dc):
        return ahead(dz, side - db, side - dc)

    partner = (me, 1 - core)
    far = range(2, planes)
    near = [(db, dc) for dc in range(side) for db in range(side) if db or dc]
    every = [(dz, db, dc) for dz in range(planes) for dc in range(side) for db in range(side)][1:]
    flat = side * side

    barrier = pltpu.get_barrier_semaphore()
    peers = [partner] + [ahead(dz, 0, 0) for dz in range(1, planes)]
    peers += [ahead(0, db, dc) for db, dc in near]
    for peer in peers:
        pl.semaphore_signal(barrier, inc=1, device_id=peer, device_id_type=MESH)

    window = max(kw, 128)
    first = pl.multiple_of((me * kw) // window * window, window)
    shift = me * kw - first
    local = [
        pltpu.make_async_copy(src, dst, l_sem.at[k])
        for k, (src, dst) in enumerate(
            (
                (feats_hbm, feats_ref),
                (pos_hbm, pos_ref),
                (waves_hbm.at[:, pl.ds(first, window)], waves_ref),
                (filt_hbm.at[pl.ds(pl.multiple_of(me * kw, kw), kw)], filt_ref),
                (mixing_hbm, mixing_ref),
                (w_in_hbm, w_in_ref),
                (w_out_hbm, w_out_ref),
                (gain_hbm, gain_ref),
            )
        )
    ]
    for copy in local[:3]:
        copy.start()

    local[0].wait()
    slot = lax.broadcasted_iota(jnp.int32, (rows, width), 0)
    live = slot < counts_ref[0]
    feats = feats_ref[...].astype(F32)
    masked = jnp.where(live, feats, 0.0).astype(BF)
    for h in range(parts):
        feat_all[h, 0] = masked[:, h * wc : (h + 1) * wc]
    local[1].wait()
    place = pos_ref[...]
    high = place.astype(BF).astype(F32)
    middle = (place - high).astype(BF).astype(F32)
    stage[...] = jnp.zeros_like(stage)
    stage[0:3, :rows] = high
    stage[3:6, :rows] = middle
    stage[6:9, :rows] = place - high - middle
    pos_all[0] = stage[:, :rows].astype(BF)

    def turned(raw):
        for part in range(3):
            stage[3 * part : 3 * part + 3, :] = raw.astype(F32)
        found = stage[...]
        if kw < window:
            found = pltpu.roll(found, (window - shift) % window, 1)
        return found.T[:kw].astype(BF)

    sent = []

    def remote(src, dst, send, recv, peer):
        copy = pltpu.make_async_remote_copy(
            src_ref=src,
            dst_ref=dst,
            send_sem=send,
            recv_sem=recv,
            device_id=peer,
            device_id_type=MESH,
        )
        copy.start()
        sent.append(copy)
        return copy

    f_copies, u_copies, p_copies = {}, {}, {}

    def send_place(src, dst, peer):
        p_copies[dst] = remote(
            pos_all.at[src], pos_all.at[dst], p_send.at[dst], p_recv.at[dst], peer
        )

    def p_begin():
        for dz in range(1, planes):
            send_place(0, dz * flat, ahead(dz, 0, 0))
        for db, dc in near:
            send_place(0, ident(0, db, dc), ahead(0, db, dc))

    def p_forward():
        for db, dc in near:
            i = ident(0, db, dc)
            p_copies[i].wait_recv()
            send_place(i, flat + i, ahead(1, 0, 0))
        for dz in far:
            p_copies[dz * flat].wait_recv()
            for db, dc in near:
                send_place(dz * flat, ident(dz, db, dc), ahead(0, db, dc))

    def send_feat(h, src, dst, peer):
        f_copies[h, dst] = remote(
            feat_all.at[h, src], feat_all.at[h, dst], f_send.at[h, dst], f_recv.at[h, dst], peer
        )

    def begin(h):
        spread(h, 0)
        for dz in (*far, 1):
            send_feat(h, 0, dz * flat, ahead(dz, 0, 0))

    def spread(h, dz):
        if dz:
            f_copies[h, dz * flat].wait_recv()
        for db, dc in near:
            send_feat(h, ident(dz, 0, 0), ident(dz, db, dc), ahead(0, db, dc))

    def across(h):
        for db, dc in near:
            f_copies[h, ident(0, db, dc)].wait_recv()
            send_feat(h, ident(0, db, dc), ident(1, db, dc), ahead(1, 0, 0))

    def core_copy(src, dst, k):
        return remote(src, dst, c_send.at[k], c_recv.at[k], partner)

    pl.semaphore_wait(barrier, len(peers))
    p_begin()
    begin(0)
    for copy in local[3:]:
        copy.start()
    local[2].wait()
    wave_copy = core_copy(waves_ref, wave_raw, 0)
    wave_own[...] = turned(waves_ref[...])
    local[3].wait()
    filt_copy = core_copy(filt_ref, filt_other, 1)
    wave_copy.wait_recv()
    wave_other[...] = turned(wave_raw[...])

    block = min(kw, 128)
    group_cols = flat * rows

    def angles(start, count):
        for k in range(start, start + count):
            if k == flat or (k > flat and k % flat):
                p_copies[k].wait_recv()
        columns = slice(start * rows, (start + count) * rows)
        spots = jnp.concatenate([pos_all[start + d] for d in range(count)], axis=1)
        for half, ref in enumerate((wave_own, wave_other)):
            base = half * 2 * kw
            for r0 in range(0, kw, block):
                turns = jnp.dot(ref[r0 : r0 + block, :], spots, preferred_element_type=F32)
                r = turns - ((turns + 12582912.0) - 12582912.0)
                zz = r * r
                s = r * horner(zz, SIN)
                co = horner(zz, COS)
                trig[base + r0 : base + r0 + block, columns] = (1.0 - s * s).astype(BF)
                trig[base + kw + r0 : base + kw + r0 + block, columns] = (s * co).astype(BF)

    step = min(2 * kw, 512)
    def part_sum(h, start, count, r0):
        columns = slice(start * rows, (start + count) * rows)
        spots = feat_all[h, start : start + count].reshape(count * rows, wc)
        return jnp.dot(trig[r0 : r0 + step, columns], spots, preferred_element_type=F32)

    def sums(h, start, count):
        for k in range(start, start + count):
            if k >= flat and (k % flat or k == flat):
                f_copies[h, k].wait_recv()
        swaps = []
        for r0 in range(0, 4 * kw, step):
            part = part_sum(h, start, count, r0)
            if start:
                part = factors[h, r0 : r0 + step, :] + part
            if start + count < n:
                factors[h, r0 : r0 + step, :] = part
            else:
                factors[h, r0 : r0 + step, :] = part
                factors_out[h, r0 : r0 + step, :] = part.astype(BF)
                if r0 + step == 4 * kw:
                    swaps.append(core_copy(factors_out.at[h], factors_in.at[h], 2 + h))
        return swaps

    scale = 1.0 / math.sqrt(atoms_all)

    def fields(h, swaps):
        for half, ref in enumerate((filt_ref, filt_other)):
            if half == 0:
                swaps[0].wait_recv()
            filt = ref[:, h * wc : (h + 1) * wc].astype(F32) * scale
            for part in range(2):
                r0 = (2 * half + part) * kw
                total = factors[h, r0 : r0 + kw, :] + factors_in[h, (r0 + 2 * kw) % (4 * kw) : (r0 + 2 * kw) % (4 * kw) + kw, :].astype(F32)
                field_t[h, :, r0 : r0 + kw] = (total * filt).astype(BF).T

    inv_k = 1.0 / math.sqrt(kwaves_all)
    pair = 2

    def start_u(h, i, peer):
        u_copies[h, i] = remote(
            send_u.at[h, i], recv_u.at[h, i], u_send.at[h, i], u_recv.at[h, i], peer
        )

    def received(h, i):
        u_copies[h, i].wait_recv()
        return recv_u[h, i].astype(F32)

    def update(h, i):
        both = jnp.dot(
            field_t[h], trig[:, i * rows : (i + pair) * rows], preferred_element_type=F32
        )
        for k in range(i, i + pair):
            dz, dc, db = k // flat, k // side % side, k % side
            block_k = both[:, (k - i) * rows : (k - i + 1) * rows]
            if dz == 1 or (dz and (db or dc)):
                send_u[h, k] = block_k.astype(BF)
                start_u(h, k, back(1, 0, 0) if dz == 1 else back(0, db, dc))
            else:
                kept[h, flat + dz if dz else k] = block_k

    def push(h):
        for k in (*range(2 * flat, 3 * flat, pair), *range(1 * flat, 2 * flat, pair), *range(3 * flat, n, pair), *range(0 * flat, 1 * flat, pair)):
            update(h, k)

    def edges_out(h):
        for db, dc in near:
            i = ident(0, db, dc)
            acc = kept[h, i] + received(h, flat + i)
            send_u[h, i] = acc.astype(BF)
            start_u(h, i, back(0, db, dc))

    def columns_out(h, planes_out):
        for dz in planes_out:
            acc = kept[h, flat + dz]
            for db, dc in near:
                acc = acc + received(h, ident(dz, db, dc))
            send_u[h, dz * flat] = acc.astype(BF)
            start_u(h, dz * flat, back(dz, 0, 0))

    def mine(h):
        acc = kept[h, 0] + received(h, flat)
        for db, dc in near:
            acc = acc + received(h, ident(0, db, dc))
        for dz in far:
            acc = acc + received(h, dz * flat)
        return acc

    for h in range(1, parts):
        begin(h)
    angles(0, 1)
    p_forward()
    for h in range(parts):
        for dz in far:
            spread(h, dz)
            if dz == 2:
                across(h)
    angles(1, 1)
    for k in range(pair, n, pair):
        angles(k, pair)
    for copy in local[4:]:
        copy.wait()
    filt_copy.wait_recv()
    for h in range(parts):
        for k in (*range(0, n - flat, flat), *range(n - flat, n)):
            swaps = sums(h, k, flat if k < n - flat else 1)
        fields(h, swaps)
        early = list(sent)
        sent.clear()
        push(h)
    for h in range(parts):
        for copy in early:
            copy.wait_send()
        columns_out(h, far[:1])
        edges_out(h)
        columns_out(h, far[1:])
    gathered = jnp.concatenate([mine(h) for h in range(parts)], axis=0)
    mixed = jnp.dot(gathered.T, mixing_ref[...], precision=HIGHEST, preferred_element_type=F32)

    state = feats + mixed * inv_k
    meansq = jnp.mean(state * state, axis=1, keepdims=True)
    normed = (state * lax.rsqrt(meansq + 1e-06) * gain_ref[...].reshape(1, width)).astype(BF)
    inner = jnp.dot(normed, w_in_ref[...], preferred_element_type=F32)
    hidden = (inner / (1.0 + jnp.exp(-inner))).astype(BF)
    result = state + jnp.dot(hidden, w_out_ref[...], preferred_element_type=F32)
    out_ref[...] = jnp.where(live, result, 0.0)

    for copy in sent:
        copy.wait_send()


def body(n, cores, positions, counts, feats, waves, wave_filter, mixing, gain, w_in, w_out):
    rows, width = feats.shape
    planes, side = grid_of(n)
    kwaves_all = waves.shape[1] * cores
    kw = waves.shape[1] // n
    wc = width // PARTS
    vmem = pl.BlockSpec(memory_space=pltpu.VMEM)
    hbm = pl.BlockSpec(memory_space=pltpu.HBM)
    held = [
        pltpu.with_memory_space_constraint(array, pltpu.HBM)
        for array in (positions, feats, waves, wave_filter, mixing, gain, w_in, w_out)
    ]
    return pl.pallas_call(
        functools.partial(kernel, n, planes, side, rows * n * cores, kwaves_all),
        out_shape=pltpu.VMEM((rows, width), F32),
        in_specs=[pl.BlockSpec(memory_space=pltpu.SMEM)]
        + [hbm] * 8,
        out_specs=vmem,
        scratch_shapes=[
            pltpu.VMEM(positions.shape, F32),
            pltpu.VMEM(feats.shape, BF),
            pltpu.VMEM((3, max(kw, 128)), waves.dtype),
            pltpu.VMEM(gain.shape, F32),
            pltpu.VMEM((kw, width), BF),
            pltpu.VMEM((kw, width), BF),
            pltpu.VMEM(mixing.shape, F32),
            pltpu.VMEM(w_in.shape, BF),
            pltpu.VMEM(w_out.shape, BF),
            pltpu.VMEM((16, max(kw, 128)), F32),
            pltpu.VMEM((kw, 16), BF),
            pltpu.VMEM((3, max(kw, 128)), waves.dtype),
            pltpu.VMEM((n, 16, rows), BF),
            pltpu.VMEM((PARTS, n, rows, wc), BF),
            pltpu.VMEM((kw, 16), BF),
            pltpu.VMEM((4 * kw, n * rows), BF),
            pltpu.VMEM((PARTS, 4 * kw, wc), F32),
            pltpu.VMEM((PARTS, 4 * kw, wc), BF),
            pltpu.VMEM((PARTS, 4 * kw, wc), BF),
            pltpu.VMEM((PARTS, wc, 4 * kw), BF),
            pltpu.VMEM((PARTS, planes + side * side, wc, rows), F32),
            pltpu.VMEM((PARTS, n, wc, rows), BF),
            pltpu.VMEM((PARTS, n, wc, rows), BF),
        ]
        + [pltpu.SemaphoreType.DMA((n,))] * 2
        + [pltpu.SemaphoreType.DMA((PARTS, n))] * 4
        + [pltpu.SemaphoreType.DMA((2 + 2 * PARTS,))] * 2
        + [pltpu.SemaphoreType.DMA((8,))],
        compiler_params=pltpu.CompilerParams(
            collective_id=0, has_side_effects=True, vmem_limit_bytes=48 * 2**20
        ),
    )(counts, *held).astype(BF)


def solution(mesh):
    n, cores = mesh.shape["atom"], mesh.shape["wave"]
    return jax.shard_map(
        functools.partial(body, n, cores),
        mesh=mesh,
        in_specs=(
            P(None, ("atom", "wave")),
            P(("atom", "wave")),
            P(("atom", "wave"), None),
            P(None, "wave"),
            P("wave", None),
            P(),
            P(),
            P(),
            P(),
        ),
        out_specs=P(("atom", "wave"), None),
        check_vma=False,
    )
```
